256 devices in a mesh: row: 8 (over y, core), col: 32 (over z, x).
Axes of the slice: x: 4, y: 4, z: 8, core: 2. Of those that a mesh axis runs over, the one named last changes fastest.
Arguments:
- solution: float32 [8, 32, 16, 128, 128], P('row', 'col'), may hold values from -6 to 6
- residual: float32 [8, 32, 16, 128, 128], P('row', 'col'), may hold values from -6 to 6, as said below
- prev_direction: float32 [8, 32, 16, 128, 128], P('row', 'col'), may hold values from -6 to 6, as said below
- prev_dot: float32 [128], replicated, may hold values from 262144 to 1048576
- face_lists: int32 [8, 32, 4, 4], P('row', 'col'), may hold values from 0 to 16, as said below
- multiplicity: int32 [8, 32, 16], P('row', 'col'), may hold values from 1 to 2, as said below
- block_pattern: int32 [8, 32, 16, 3], P('row', 'col'), may hold values from 0 to 15, as said below
- schur: float32 [8, 32, 16, 3, 128, 128], P('row', 'col'), may hold values from -1 to 4, as said below
- neumann_inverse: float32 [8, 32, 16, 3, 128, 128], P('row', 'col'), may hold values from 0 to 2, as said below
- coarse_basis: float32 [8, 32, 8, 2048], P('row', 'col'), may hold values from -0.25 to 0.25
- primal_map: int32 [8, 32, 8], P('row', 'col'), may hold values from 0 to 1023, all different within a row
- coarse_inverse: float32 [1024, 1024], P('col'), may hold values from -1 to 1, as said below
Outputs:
- new_solution: float32 [8, 32, 16, 128, 128], P('row', 'col')
- new_residual: float32 [8, 32, 16, 128, 128], P('row', 'col')
- direction: float32 [8, 32, 16, 128, 128], P('row', 'col')
The draws below stay inside these ranges and needn't reach their ends.
Inputs may be any that keep to these rules, and one draw needn't show every extreme that they name: face_lists[i, j, f, k] names the interface blocks that subdomain (i, j) shares with its neighbour across face f (0 toward row i-1, 1 toward row i+1, 2 toward column j-1, 3 toward column j+1); slot k of a face names the same unknowns as slot k of the neighbour's list for the facing face, and both lists have the same length, 1 to 4 blocks, none on faces at the grid's edge; unused slots hold 16; no block lies on two faces; some face holds 4 blocks. multiplicity is 2 for blocks named in face_lists and 1 for the others. block_pattern[i, j, b, 0] = b; the two other entries of block row b are two other blocks, each of which lists b in turn. `schur`: each subdomain's Schur complement is symmetric positive definite, with positive diagonal and no positive entry off it. `neumann_inverse`: each subdomain's local solve matrix is symmetric positive definite. `coarse_inverse`: symmetric positive definite. `residual`: copies of an unknown held by two subdomains (slot k of facing lists) are equal. `prev_direction`: copies of an unknown held by two subdomains (slot k of facing lists) are equal.
All inputs are finite; a program needn't handle non-finite values.
Results may differ from the reference program's by a relative error of at most 0.0003.
Values sent between devices are 32-bit elements; how exact they have to be, the bound alone decides.
A program may use at most 128 MiB of HBM per device.

```python
import math
import jax
import jax.numpy as jnp
from jax import lax

BLOCKS = 16
BLOCK_DOFS = 128
FACE_SLOTS = 4
LOAD_CASES = 128
PRIMALS = 8
SUB_ROWS = 8
SUB_COLS = 32
COARSE_ROWS = 1024


def face_layout(key):
    base = jax.random.fold_in(key, 7001)
    first_key, second_key, third_key = jax.random.split(base, 3)
    rows_len = jax.random.randint(first_key, (SUB_ROWS - 1, SUB_COLS), 1, FACE_SLOTS + 1)
    rows_len = rows_len.at[0, 0].set(FACE_SLOTS)
    cols_len = jax.random.randint(second_key, (SUB_ROWS, SUB_COLS - 1), 1, FACE_SLOTS + 1)
    cols_len = cols_len.at[0, 0].set(FACE_SLOTS)
    zero_row = jnp.zeros((1, SUB_COLS), jnp.int32)
    zero_col = jnp.zeros((SUB_ROWS, 1), jnp.int32)
    north = jnp.concatenate([zero_row, rows_len], axis=0)
    south = jnp.concatenate([rows_len, zero_row], axis=0)
    west = jnp.concatenate([zero_col, cols_len], axis=1)
    east = jnp.concatenate([cols_len, zero_col], axis=1)
    lengths = jnp.stack([north, south, west, east], axis=-1).astype(jnp.int32)
    starts = jnp.cumsum(lengths, axis=-1) - lengths
    scores = jax.random.randint(third_key, (SUB_ROWS, SUB_COLS, BLOCKS), 0, 1 << 20) * BLOCKS + jnp.arange(BLOCKS)
    order = jnp.argsort(scores, axis=-1).astype(jnp.int32)
    slots = jnp.arange(FACE_SLOTS).astype(jnp.int32)
    position = jnp.minimum(starts[..., None] + slots, BLOCKS - 1)
    picked = jnp.take_along_axis(order, position.reshape(SUB_ROWS, SUB_COLS, 4 * FACE_SLOTS), axis=-1)
    picked = picked.reshape(SUB_ROWS, SUB_COLS, 4, FACE_SLOTS)
    return jnp.where(slots < lengths[..., None], picked, BLOCKS).astype(jnp.int32)


def pattern_layout(key):
    base = jax.random.fold_in(key, 7002)
    scores = jax.random.randint(base, (SUB_ROWS, SUB_COLS, BLOCKS), 0, 1 << 20) * BLOCKS + jnp.arange(BLOCKS)
    order = jnp.argsort(scores, axis=-1).astype(jnp.int32)
    position = jnp.argsort(order, axis=-1).astype(jnp.int32)
    next_block = jnp.take_along_axis(order, (position + 1) % BLOCKS, axis=-1)
    prev_block = jnp.take_along_axis(order, (position + BLOCKS - 1) % BLOCKS, axis=-1)
    own_block = jnp.broadcast_to(jnp.arange(BLOCKS).astype(jnp.int32), next_block.shape)
    return jnp.stack([own_block, next_block, prev_block], axis=-1).astype(jnp.int32)


def draw_face_lists(key, part):
    return face_layout(key)


def draw_multiplicity(key, part):
    faces = face_layout(key)
    named = (faces[..., None] == jnp.arange(BLOCKS)).astype(jnp.int32)
    return (1 + jnp.sum(named, axis=(2, 3))).astype(jnp.int32)


def draw_block_pattern(key, part):
    return pattern_layout(key)


def symmetric_blocks(key, salt, lower, upper, diag_lower, diag_upper):
    pattern = pattern_layout(key)
    base = jax.random.fold_in(key, salt)
    first_key, second_key = jax.random.split(base)
    shape = (SUB_ROWS, SUB_COLS, BLOCKS, 3, BLOCK_DOFS, BLOCK_DOFS)
    uniform_draw = jax.random.uniform(first_key, shape, jnp.float32)
    random_draw = lower + (upper - lower) * uniform_draw
    subdomain = (jnp.arange(SUB_ROWS * SUB_COLS).reshape(SUB_ROWS, SUB_COLS, 1) * BLOCKS).astype(jnp.int32)
    flat_next = random_draw[:, :, :, 2].reshape(SUB_ROWS * SUB_COLS * BLOCKS, BLOCK_DOFS, BLOCK_DOFS)
    flat_prev = random_draw[:, :, :, 1].reshape(SUB_ROWS * SUB_COLS * BLOCKS, BLOCK_DOFS, BLOCK_DOFS)
    from_next = jnp.take(flat_next, (subdomain + pattern[..., 1]).reshape(-1), axis=0)
    from_prev = jnp.take(flat_prev, (subdomain + pattern[..., 2]).reshape(-1), axis=0)
    from_next = from_next.reshape(SUB_ROWS, SUB_COLS, BLOCKS, BLOCK_DOFS, BLOCK_DOFS)
    from_prev = from_prev.reshape(SUB_ROWS, SUB_COLS, BLOCKS, BLOCK_DOFS, BLOCK_DOFS)
    block_next = (random_draw[:, :, :, 1] + jnp.swapaxes(from_next, -1, -2)) * 0.5
    block_prev = (random_draw[:, :, :, 2] + jnp.swapaxes(from_prev, -1, -2)) * 0.5
    diagonal_block = (random_draw[:, :, :, 0] + jnp.swapaxes(random_draw[:, :, :, 0], -1, -2)) * 0.5
    log_values = jax.random.uniform(second_key, (SUB_ROWS, SUB_COLS, BLOCKS, BLOCK_DOFS), jnp.float32, jnp.log(diag_lower), jnp.log(diag_upper))
    diag_values = jnp.exp(log_values)
    identity = jnp.eye(BLOCK_DOFS, dtype=jnp.float32)
    diagonal_block = diagonal_block * (1.0 - identity) + diag_values[..., None] * identity
    return jnp.stack([diagonal_block, block_next, block_prev], axis=3)


def draw_schur(key, part):
    blocks = symmetric_blocks(key, 7003, -2.0 / (3 * BLOCK_DOFS), 0.0, 0.05, 2.0)
    identity = jnp.eye(BLOCK_DOFS, dtype=jnp.float32)
    shift = jnp.zeros((3, 1, 1), jnp.float32).at[0].set(2.0)
    return blocks + shift * identity


def draw_neumann_inverse(key, part):
    return symmetric_blocks(key, 7004, 0.0, 0.5 / (3 * BLOCK_DOFS), 0.6, 2.0)


def draw_coarse_inverse(key, part):
    base = jax.random.fold_in(key, 7005)
    first_key, second_key = jax.random.split(base)
    bound_value = 0.2 / COARSE_ROWS
    random_draw = jax.random.uniform(first_key, (COARSE_ROWS, COARSE_ROWS), jnp.float32, -bound_value, bound_value)
    symmetric = (random_draw + random_draw.T) * 0.5
    diag_values = jnp.exp(jax.random.uniform(second_key, (COARSE_ROWS,), jnp.float32, jnp.log(0.25), 0.0))
    identity = jnp.eye(COARSE_ROWS, dtype=jnp.float32)
    return symmetric * (1.0 - identity) + diag_values[:, None] * identity


def matched_field(key, salt):
    faces = face_layout(key)
    base = jax.random.fold_in(key, salt)
    shape = (SUB_ROWS, SUB_COLS, BLOCKS, BLOCK_DOFS, LOAD_CASES)
    random_draw = jnp.clip(jax.random.normal(base, shape, jnp.float32), -6.0, 6.0)
    subdomain = (jnp.arange(SUB_ROWS * SUB_COLS).reshape(SUB_ROWS, SUB_COLS, 1) * BLOCKS).astype(jnp.int32)
    result = random_draw
    for axis_number, mine_face, their_face in ((0, 0, 1), (1, 2, 3)):
        neighbour = jnp.roll(random_draw, 1, axis=axis_number).reshape(SUB_ROWS * SUB_COLS * BLOCKS, BLOCK_DOFS, LOAD_CASES)
        their_list = jnp.minimum(jnp.roll(faces[:, :, their_face], 1, axis=axis_number), BLOCKS - 1)
        incoming = jnp.take(neighbour, (subdomain + their_list).reshape(-1), axis=0)
        incoming = incoming.reshape(SUB_ROWS, SUB_COLS, FACE_SLOTS, BLOCK_DOFS, LOAD_CASES)
        mine_list = faces[:, :, mine_face]
        for slot_number in range(FACE_SLOTS):
            chosen = mine_list[:, :, slot_number][..., None] == jnp.arange(BLOCKS)
            result = jnp.where(chosen[..., None, None], incoming[:, :, slot_number][:, :, None], result)
    return result


def draw_residual(key, part):
    return matched_field(key, 7010)


def draw_prev_direction(key, part):
    return matched_field(key, 7011)


def shard_levels(own_key, extent, pieces, least, largest):
    loudness = 1.0
    for dim, shards_of in pieces:
        steps = jax.random.uniform(jax.random.fold_in(jax.random.fold_in(own_key, 6), dim), (shards_of,), jnp.float32, least / len(pieces), largest / len(pieces))
        loudness = loudness * jnp.repeat(jnp.exp(steps), extent[dim] // shards_of).reshape((-1,) + (1,) * (len(extent) - 1 - dim))
    return loudness


def picks_of(stream_key, rows, number_of, top, lift):
    order = jax.random.permutation(jax.random.fold_in(stream_key, 1), number_of)
    favour = order
    for power in range(3):
        favour = favour * favour // number_of
    favour = favour * lift // number_of
    chance = jax.random.randint(jax.random.fold_in(stream_key, 2), (rows, number_of), 0, 4096) + favour
    fixed_rows = jax.random.permutation(jax.random.fold_in(stream_key, 3), rows)[jnp.arange(number_of) % rows]
    chance = jnp.where(jnp.arange(rows)[:, None] == fixed_rows[None, :], 1 << 14, chance)
    priority = chance * number_of + jnp.arange(number_of)
    return lax.top_k(priority.astype(jnp.int32), top)[1].astype(jnp.int32)


def bell_draw(rng, shape, deviation, reach, shards=(), kind=jnp.bfloat16):
    level = shard_levels(rng, shape, shards, -0.22, 0.18) if shards else 1.0
    drawn = jax.random.normal(rng, shape, jnp.float32) * deviation * level
    return jnp.minimum(jnp.maximum(drawn, -reach), reach).astype(kind)


def setup_inputs(seed: int = 0) -> dict:
    streams_of = jax.random.split(jax.random.key(seed), 13)
    solution = bell_draw(streams_of[0], (SUB_ROWS, SUB_COLS, BLOCKS, BLOCK_DOFS, LOAD_CASES), 1.0, 6.0, ((0, 8), (1, 32)), jnp.float32)
    residual = draw_residual(jax.random.fold_in(streams_of[12], 71), 0)
    prev_direction = draw_prev_direction(jax.random.fold_in(streams_of[12], 71), 0)
    prev_dot = jnp.clip(jnp.exp(jax.random.uniform(streams_of[3], (LOAD_CASES,), jnp.float32, math.log(262144.0), math.log(1048576))), 262144.0, 1048576)
    face_lists = draw_face_lists(jax.random.fold_in(streams_of[12], 71), 0)
    multiplicity = draw_multiplicity(jax.random.fold_in(streams_of[12], 71), 0)
    block_pattern = draw_block_pattern(jax.random.fold_in(streams_of[12], 71), 0)
    schur = draw_schur(jax.random.fold_in(streams_of[12], 71), 0)
    neumann_inverse = draw_neumann_inverse(jax.random.fold_in(streams_of[12], 71), 0)
    coarse_basis = bell_draw(streams_of[9], (SUB_ROWS, SUB_COLS, PRIMALS, BLOCKS * BLOCK_DOFS), (BLOCKS * BLOCK_DOFS // 4) ** -0.5, 0.25, ((0, 8), (1, 32)), jnp.float32)
    primal_map = picks_of(streams_of[10], SUB_ROWS * SUB_COLS, COARSE_ROWS, PRIMALS, 64).reshape((SUB_ROWS, SUB_COLS, PRIMALS))
    coarse_inverse = draw_coarse_inverse(jax.random.fold_in(streams_of[12], 71), 0)
    return {"solution": solution, "residual": residual, "prev_direction": prev_direction, "prev_dot": prev_dot, "face_lists": face_lists, "multiplicity": multiplicity, "block_pattern": block_pattern, "schur": schur, "neumann_inverse": neumann_inverse, "coarse_basis": coarse_basis, "primal_map": primal_map, "coarse_inverse": coarse_inverse}


HIGH = lax.Precision.HIGHEST


def apply_blocks(blocks, pattern, values_in):
    def one_row(packed):
        row_blocks, row_pattern, row_values = packed
        columns = row_pattern.shape[0]
        count = row_pattern.shape[1] * row_pattern.shape[2]
        index = row_pattern.reshape(columns, count)[:, :, None, None]
        gathered = jnp.take_along_axis(row_values, index, axis=1)
        gathered = gathered.reshape(row_blocks.shape[:3] + row_values.shape[2:])
        return jnp.einsum("sbkij,sbkjn->sbin", row_blocks, gathered, precision=HIGH)
    return lax.map(one_row, (blocks, pattern, values_in))


def assemble(values_in, face_lists):
    blocks = values_in.shape[2]
    indicator = (face_lists[..., None] == jnp.arange(blocks)).astype(jnp.float32)
    face_values = jnp.einsum("ijfkb,ijbcn->ijfkcn", indicator, values_in, precision=HIGH)
    zero_row = jnp.zeros_like(face_values[:1, :, 0])
    from_north = jnp.concatenate([zero_row, face_values[:-1, :, 1]], axis=0)
    from_south = jnp.concatenate([face_values[1:, :, 0], zero_row], axis=0)
    zero_col = jnp.zeros_like(face_values[:, :1, 2])
    from_west = jnp.concatenate([zero_col, face_values[:, :-1, 3]], axis=1)
    from_east = jnp.concatenate([face_values[:, 1:, 2], zero_col], axis=1)
    received = jnp.stack([from_north, from_south, from_west, from_east], axis=2)
    return values_in + jnp.einsum("ijfkb,ijfkcn->ijbcn", indicator, received, precision=HIGH)


def reference(solution, residual, prev_direction, prev_dot, face_lists, multiplicity, block_pattern, schur, neumann_inverse, coarse_basis, primal_map, coarse_inverse):
    weight = (1.0 / multiplicity.astype(jnp.float32))[..., None, None]
    scaled = residual * weight
    local_term = apply_blocks(neumann_inverse, block_pattern, scaled)
    sub_rows, sub_cols, blocks, dofs, cases = residual.shape
    flattened = scaled.reshape(sub_rows, sub_cols, blocks * dofs, cases)
    coarse_local = jnp.einsum("ijpd,ijdn->ijpn", coarse_basis, flattened, precision=HIGH)
    indicator = (primal_map[..., None] == jnp.arange(coarse_inverse.shape[0])).astype(jnp.float32)
    coarse_rhs = jnp.einsum("ijpc,ijpn->cn", indicator, coarse_local, precision=HIGH)
    coarse_sol = jnp.dot(coarse_inverse, coarse_rhs, precision=HIGH)
    own_coarse = jnp.einsum("ijpc,cn->ijpn", indicator, coarse_sol, precision=HIGH)
    coarse_back = jnp.einsum("ijpd,ijpn->ijdn", coarse_basis, own_coarse, precision=HIGH)
    coarse_back = coarse_back.reshape(residual.shape)
    precond = assemble((local_term + coarse_back) * weight, face_lists)
    precond_dot = jnp.sum(residual * precond * weight, axis=(0, 1, 2, 3))
    direction = precond + (precond_dot / prev_dot) * prev_direction
    image = assemble(apply_blocks(schur, block_pattern, direction), face_lists)
    curvature = jnp.sum(direction * image * weight, axis=(0, 1, 2, 3))
    step_size = precond_dot / curvature
    return solution + step_size * direction, residual - step_size * image, direction
```

```python
import jax
import jax.numpy as jnp
from jax import lax
from jax.experimental import pallas as pl
from jax.experimental.pallas import tpu as pltpu
from jax.sharding import PartitionSpec as P

MESH = pl.DeviceIdType.MESH
F32 = jnp.float32
BF16 = jnp.bfloat16
ROWS, COLS = 8, 32
BLOCKS, DOFS, CASES, SLOTS, PRIMALS = 16, 128, 128, 4, 8
OWNED = 32
COARSE = OWNED * COLS
OPPOSITE = (1, 0, 3, 2)


def split(values):
    high = values.astype(BF16)
    return high, (values - high.astype(F32)).astype(BF16)


def mm(left, right):
    return jnp.dot(left, right, preferred_element_type=F32)


def wide(values):
    return jnp.concatenate(split(values), axis=1)


def iteration(
    faces, pattern, mult, pmap,
    residual_h, previous_h, solution_h, prev_dot, schur_h, neumann_h, basis_h, inverse_h,
    new_solution_h, new_residual_h, direction_h,
    nonface, sigma, place, slot_pat,
    residual, previous, solution, schur, neumann, basis, tiles, inverse,
    scaled, local, schur_hi, schur_lo, lifted, spread, chosen, picker,
    direct, direct_hl, image, out_dir, out_res,
    map_own, map_got, near_own, near_got,
    face_basis, got_basis, got_local, got_image,
    a_buf, b_own, b_got, c_buf, e_own, e_got, coarse, v_buf, w_own, w_got,
    load_sem, store_sem, send_sem, recv_sem, face_send, face_recv,
):
    i = lax.axis_index("row")
    j = lax.axis_index("col")
    row_id = lambda t: (lax.rem(i + t, ROWS), j)
    col_id = lambda t: (i, lax.rem(j + t, COLS))
    face_id = (row_id(ROWS - 1), row_id(1), col_id(COLS - 1), col_id(1))

    loads = []
    for n, (source, target) in enumerate(
        (
            (residual_h, residual), (basis_h, basis), (inverse_h, inverse), (neumann_h, neumann),
            (schur_h, schur), (previous_h, previous), (solution_h, solution),
        )
    ):
        loads.append(pltpu.make_async_copy(source, target, load_sem.at[n]))
        loads[-1].start()
    got_residual, got_basis_own, got_inverse, got_neumann, got_schur, got_previous, got_solution = loads

    barrier = pltpu.get_barrier_semaphore()

    def greet_col(t, carry):
        pl.semaphore_signal(barrier, inc=1, device_id=col_id(t), device_id_type=MESH)
        return carry

    def greet_row(t, carry):
        pl.semaphore_signal(barrier, inc=1, device_id=row_id(t), device_id_type=MESH)
        return carry

    lax.fori_loop(1, COLS, greet_col, 0)
    lax.fori_loop(1, ROWS, greet_row, 0)

    def gather_col(buffer, stage):
        def send(t, carry):
            pltpu.make_async_remote_copy(
                src_ref=buffer.at[j], dst_ref=buffer.at[j], send_sem=send_sem.at[stage], recv_sem=recv_sem.at[stage],
                device_id=col_id(t), device_id_type=MESH,
            ).start()
            return carry

        lax.fori_loop(1, COLS, send, 0)

    def scatter_row(own, got, stage, whole):
        def send(t, carry):
            source = own if whole else own.at[lax.rem(i + t, ROWS)]
            pltpu.make_async_remote_copy(
                src_ref=source, dst_ref=got.at[i], send_sem=send_sem.at[stage], recv_sem=recv_sem.at[stage],
                device_id=row_id(t), device_id_type=MESH,
            ).start()
            return carry

        lax.fori_loop(1, ROWS, send, 0)

    def await_bytes(buffer, count, sem):
        view = buffer.at[pl.ds(0, count)]
        pltpu.make_async_copy(view, view, sem).wait()

    def send_face(own, got, face, group):
        pltpu.make_async_remote_copy(
            src_ref=own, dst_ref=got.at[OPPOSITE[face]],
            send_sem=face_send.at[group, face], recv_sem=face_recv.at[group, OPPOSITE[face]],
            device_id=face_id[face], device_id_type=MESH,
        ).start()

    def find_nonface(b, count):
        on_face = faces[0, 0] == b
        for s in range(1, 16):
            on_face = jnp.logical_or(on_face, faces[s // 4, s % 4] == b)
        nonface[b] = jnp.where(on_face, -1, count)
        return count + jnp.where(on_face, 0, 1)

    lax.fori_loop(0, BLOCKS, find_nonface, jnp.int32(0))

    def find_sigma(s, count):
        named = faces[s // 4, s % 4]
        free = named >= BLOCKS
        block = jnp.int32(0)
        for b in range(BLOCKS):
            block = jnp.where(nonface[b] == count, b, block)
        sigma[s] = jnp.where(free, block, named)
        return count + jnp.where(free, 1, 0)

    lax.fori_loop(0, BLOCKS, find_sigma, jnp.int32(0))

    def find_place(b, carry):
        slot = jnp.int32(0)
        for s in range(BLOCKS):
            slot = jnp.where(sigma[s] == b, s, slot)
        place[b] = slot
        return carry

    lax.fori_loop(0, BLOCKS, find_place, 0)

    def find_slot_pat(s, carry):
        for k in range(3):
            slot_pat[s, k] = place[pattern[sigma[s], k]]
        return carry

    lax.fori_loop(0, BLOCKS, find_slot_pat, 0)

    weight = lambda b: jnp.where(mult[b] == 2, F32(0.5), F32(1.0))
    used = lambda s: jnp.where(faces[s // 4, s % 4] < BLOCKS, F32(1.0), F32(0.0))

    lanes = lax.broadcasted_iota(jnp.int32, (1, 128), 1)
    own_map = jnp.zeros((1, 128), jnp.int32)
    for p in range(PRIMALS):
        own_map = jnp.where(lax.rem(lanes, 8) == p, pmap[p], own_map)
    map_own[...] = own_map.astype(F32)
    map_got[j] = map_own[...]

    pl.semaphore_wait(barrier, COLS - 1 + ROWS - 1)

    gather_col(map_got, 0)

    got_residual.wait()
    got_basis_own.wait()

    def scale(b, carry):
        scaled[b] = wide(residual[b] * weight(b))
        return carry

    lax.fori_loop(0, BLOCKS, scale, 0, unroll=2)
    basis_hi, basis_lo = split(basis[...])
    both = mm(jnp.concatenate([basis_hi, basis_lo], axis=0), scaled[...].reshape(BLOCKS * DOFS, 2 * CASES))
    a_buf[j] = both[0:8, 0:CASES] + both[0:8, CASES:] + both[8:16, 0:CASES]
    gather_col(a_buf, 1)

    for b in range(BLOCKS):
        tiles[b] = basis[:, b * DOFS : (b + 1) * DOFS]
    for face in (2, 3, 0, 1):
        for k in range(SLOTS):
            b = sigma[face * 4 + k]
            face_basis[face, k] = tiles[b]
        send_face(face_basis.at[face], got_basis, face, 0)

    got_neumann.wait()

    def local_row(s, dot):
        b = sigma[s]
        blocks = jnp.concatenate([neumann[b, k] for k in range(3)], axis=1)
        high, low = split(blocks)
        values = jnp.concatenate([scaled[pattern[b, k]] for k in range(3)], axis=0)
        both = mm(high, values)
        row = both[:, 0:CASES] + both[:, CASES:] + mm(low, values[:, 0:CASES])
        row = row * weight(b)
        local[s // 4, lax.rem(s, 4)] = row
        return dot + jnp.sum((residual[b] * row).reshape(16, 8, CASES), axis=0)

    local_dot = lax.fori_loop(0, BLOCKS, local_row, jnp.zeros((8, CASES), F32), unroll=2)
    local_dot = jnp.sum(local_dot, axis=0, keepdims=True)
    for face in (2, 3, 0, 1):
        send_face(local.at[face], got_local, face, 1)

    await_bytes(map_got, COLS - 1, recv_sem.at[0])
    group = lanes // 8
    code = jnp.where(lax.rem(lanes, 8) == 0, F32(-1.0), F32(-2.0))
    west = map_got[lax.rem(j + COLS - 1, COLS)]
    east = map_got[lax.rem(j + 1, COLS)]
    quarter = lax.rem(group, 4)
    near_own[...] = jnp.where(quarter == 0, map_got[j], jnp.where(quarter == 1, west, jnp.where(quarter == 2, east, code)))
    near_got[i] = near_own[...]
    scatter_row(near_own, near_got, 2, True)
    halves = []
    for half in range(2):
        line = jnp.zeros((1, 128), F32)
        for t in range(16):
            line = jnp.where(group == t, map_got[half * 16 + t], line)
        halves.append(line.astype(jnp.int32))
    entries = jnp.concatenate(halves, axis=1)
    got_inverse.wait()

    def pick(c, total):
        rows = lax.broadcasted_iota(jnp.int32, (256, 256), 0) + c * 256
        hot = jnp.where(rows == entries, F32(1.0), F32(0.0)).astype(BF16)
        return total + mm(wide_rows(inverse[:, pl.ds(pl.multiple_of(c * 256, 256), 256)]), hot)

    wide_rows = lambda values: jnp.concatenate(split(values), axis=0)
    total = lax.fori_loop(0, COARSE // 256, pick, jnp.zeros((2 * OWNED, 256), F32))
    columns_hi, columns_lo = split(total[0:OWNED] + total[OWNED:])
    rows = lax.broadcasted_iota(jnp.int32, (64, OWNED), 0)
    cols = lax.broadcasted_iota(jnp.int32, (64, OWNED), 1)
    spot = (rows // 8) * 4 + lax.rem(rows, 4)
    first = lax.rem(rows, 8) < 4
    order = jnp.where(jnp.logical_and(first, spot == cols), F32(1.0), F32(0.0)).astype(BF16)
    rows = lax.broadcasted_iota(jnp.int32, (64, 256), 0)
    spot = (rows // 8) * 4 + lax.rem(rows, 4) + j * OWNED
    first = lax.rem(rows, 8) < 4
    own_hot = jnp.where(jnp.logical_and(jnp.logical_not(first), spot == entries), F32(1.0), F32(0.0))
    chosen[0:64] = (mm(order, columns_hi) + own_hot).astype(BF16)
    chosen[64:128] = mm(order, columns_lo).astype(BF16)

    await_bytes(a_buf, COLS - 1, recv_sem.at[1])
    both = mm(chosen[...], wide(a_buf[...].reshape(COLS * PRIMALS, CASES)))
    parts = both[0:64, 0:CASES] + both[0:64, CASES:] + both[64:128, 0:CASES]
    b_own[...] = parts.reshape(ROWS, 8, CASES)
    b_got[i] = b_own[i]
    scatter_row(b_own, b_got, 3, False)

    await_bytes(near_got, ROWS - 1, recv_sem.at[2])
    for half in range(2):
        line = jnp.zeros((1, 128), F32)
        for t in range(4):
            line = jnp.where(lanes // 32 == t, near_got[half * 4 + t], line)
        line = line.astype(jnp.int32)
        here = jnp.logical_and(line >= 0, lax.rem(line // 4, 8) == i)
        where_at = jnp.where(here, (line // OWNED) * 8 + lax.rem(line, 4), -1)
        for quarter_rows in range(2):
            rows = lax.broadcasted_iota(jnp.int32, (128, 128), 0) + quarter_rows * 128
            hit = jnp.logical_or(rows == where_at, jnp.logical_and(line == -1, lax.rem(rows, 8) == 4))
            hot = jnp.where(hit, F32(1.0), F32(0.0))
            picker[pl.ds(half * 128, 128), pl.ds(quarter_rows * 128, 128)] = jnp.transpose(hot).astype(BF16)

    await_bytes(b_got, ROWS - 1, recv_sem.at[3])
    held = jnp.sum(b_got[...], axis=0)
    dot = 0.5 * jnp.sum(held * pltpu.roll(held, 4, 0), axis=0, keepdims=True) + local_dot
    rows = lax.broadcasted_iota(jnp.int32, (8, CASES), 0)
    c_buf[j] = jnp.where(rows < 4, held, jnp.where(rows == 4, jnp.broadcast_to(dot, (8, CASES)), F32(0.0)))
    gather_col(c_buf, 4)

    got_schur.wait()

    def order_schur(s, carry):
        b = sigma[s]
        high, low = split(jnp.concatenate([schur[b, k] for k in range(3)], axis=1))
        schur_hi[s] = high
        schur_lo[s] = low
        return carry

    lax.fori_loop(0, BLOCKS, order_schur, 0)

    for face in range(4):
        await_bytes(got_basis.at[face], SLOTS, face_recv.at[0, face])

    def lift(s, carry):
        b = sigma[s]
        own = tiles[b]
        other = got_basis[s // 4, lax.rem(s, 4)] * used(s)
        stack = jnp.concatenate([own, other], axis=0) * weight(b)
        high, low = split(stack)
        high = high.astype(F32)
        full = jnp.concatenate([high, high, low.astype(F32), jnp.zeros((80, DOFS), F32)], axis=0)
        lifted[s] = jnp.transpose(full).astype(BF16)
        return carry

    lax.fori_loop(0, BLOCKS, lift, 0)

    for face in range(4):
        await_bytes(got_local.at[face], SLOTS, face_recv.at[1, face])
        await_bytes(local.at[face], SLOTS, face_send.at[1, face])

    def add_faces(s, carry):
        local[s // 4, lax.rem(s, 4)] = local[s // 4, lax.rem(s, 4)] + used(s) * got_local[s // 4, lax.rem(s, 4)]
        return carry

    lax.fori_loop(0, BLOCKS, add_faces, 0)
    got_previous.wait()

    await_bytes(c_buf, COLS - 1, recv_sem.at[4])
    both = mm(picker[...], wide(c_buf[...].reshape(COLS * 8, CASES)))
    spread[...] = (both[:, 0:CASES] + both[:, CASES:]).reshape(ROWS, 32, CASES)
    for t in range(ROWS):
        e_own[t, 0:8] = spread[t, 0:8]
        e_own[t, 8:16] = spread[(t + 7) % ROWS, 0:8]
        e_own[t, 16:24] = spread[(t + 1) % ROWS, 0:8]
        e_own[t, 24:48] = spread[t, 8:32]
    e_got[i] = e_own[i]
    scatter_row(e_own, e_got, 5, False)
    await_bytes(e_got, ROWS - 1, recv_sem.at[5])
    coarse[...] = jnp.sum(e_got[...], axis=0)
    precond_dot = coarse[40:41]
    mix = precond_dot / prev_dot[...]

    for face in range(4):
        stack = jnp.concatenate([coarse[0:8], coarse[8 + 8 * face : 16 + 8 * face]], axis=0)
        high, low = split(stack)
        high = high.astype(F32)
        right = jnp.concatenate([high, low.astype(F32), high, jnp.zeros((80, CASES), F32)], axis=0).astype(BF16)
        for k in range(SLOTS):
            s = face * 4 + k
            value = local[face, k] + mm(lifted[s], right) + mix * previous[sigma[s]]
            direct[s] = value
            direct_hl[s] = wide(value)

    total = jnp.zeros((8, CASES), F32)
    for face in (2, 3, 0, 1):
        def image_row(k, total):
            s = face * 4 + k
            values = jnp.concatenate([direct_hl[slot_pat[s, n]] for n in range(3)], axis=0)
            both = mm(schur_hi[s], values)
            row = both[:, 0:CASES] + both[:, CASES:] + mm(schur_lo[s], values[:, 0:CASES])
            image[face, k] = row
            return total + jnp.sum((direct[s] * row).reshape(16, 8, CASES), axis=0)

        total = lax.fori_loop(0, SLOTS, image_row, total, unroll=2)
        send_face(image.at[face], got_image, face, 2)

    v_buf[j] = jnp.sum(total, axis=0, keepdims=True)
    gather_col(v_buf, 6)

    def order_direction(b, carry):
        out_dir[b] = direct[place[b]]
        return carry

    lax.fori_loop(0, BLOCKS, order_direction, 0)
    store_direction = pltpu.make_async_copy(out_dir, direction_h, store_sem.at[0])
    store_direction.start()
    got_solution.wait()

    await_bytes(v_buf, COLS - 1, recv_sem.at[6])
    w_own[...] = jnp.sum(v_buf[...], axis=0)
    w_got[i] = w_own[...]
    scatter_row(w_own, w_got, 7, True)
    await_bytes(w_got, ROWS - 1, recv_sem.at[7])
    step_size = precond_dot / jnp.sum(w_got[...], axis=0)

    def move(b, carry):
        solution[b] = solution[b] + step_size * out_dir[b]
        return carry

    lax.fori_loop(0, BLOCKS, move, 0)
    store_solution = pltpu.make_async_copy(solution, new_solution_h, store_sem.at[1])
    store_solution.start()

    for face in range(4):
        await_bytes(got_image.at[face], SLOTS, face_recv.at[2, face])

    def finish(b, carry):
        s = place[b]
        full = image[s // 4, lax.rem(s, 4)] + used(s) * got_image[s // 4, lax.rem(s, 4)]
        out_res[b] = residual[b] - step_size * full
        return carry

    lax.fori_loop(0, BLOCKS, finish, 0)
    store_residual = pltpu.make_async_copy(out_res, new_residual_h, store_sem.at[2])
    store_residual.start()

    for buffer, stage in ((map_got, 0), (a_buf, 1), (c_buf, 4), (v_buf, 6)):
        await_bytes(buffer, COLS - 1, send_sem.at[stage])
    for buffer, stage in ((near_got, 2), (b_got, 3), (e_got, 5), (w_got, 7)):
        await_bytes(buffer, ROWS - 1, send_sem.at[stage])
    for face in range(4):
        await_bytes(face_basis.at[face], SLOTS, face_send.at[0, face])
        await_bytes(image.at[face], SLOTS, face_send.at[2, face])
    store_direction.wait()
    store_solution.wait()
    store_residual.wait()


def per_device(
    solution, residual, prev_direction, prev_dot, face_lists, multiplicity, block_pattern,
    schur, neumann_inverse, coarse_basis, primal_map, coarse_inverse,
):
    field = jax.ShapeDtypeStruct((BLOCKS, DOFS, CASES), F32)
    smem = pl.BlockSpec(memory_space=pltpu.SMEM)
    hbm = pl.BlockSpec(memory_space=pl.ANY)
    vmem = pl.BlockSpec(memory_space=pltpu.VMEM)
    V = pltpu.VMEM
    tall = (4, SLOTS, DOFS, CASES)
    outs = pl.pallas_call(
        iteration,
        out_shape=(field, field, field),
        in_specs=[smem] * 4 + [hbm] * 3 + [vmem] + [hbm] * 4,
        out_specs=(hbm, hbm, hbm),
        scratch_shapes=[
            pltpu.SMEM((16,), jnp.int32), pltpu.SMEM((16,), jnp.int32), pltpu.SMEM((16,), jnp.int32),
            pltpu.SMEM((16, 3), jnp.int32),
            V((16, 128, 128), F32), V((16, 128, 128), F32), V((16, 128, 128), F32),
            V((16, 3, 128, 128), F32), V((16, 3, 128, 128), F32), V((8, 2048), F32), V((16, 8, 128), F32), V((32, 1024), F32),
            V((16, 128, 256), BF16), V(tall, F32), V((16, 128, 384), BF16), V((16, 128, 384), BF16),
            V((16, 128, 128), BF16), V((8, 32, 128), F32), V((128, 256), BF16), V((256, 256), BF16),
            V((16, 128, 128), F32), V((16, 128, 256), BF16), V(tall, F32), V((16, 128, 128), F32), V((16, 128, 128), F32),
            V((1, 128), F32), V((32, 1, 128), F32), V((1, 128), F32), V((8, 1, 128), F32),
            V((4, 4, 8, 128), F32), V((4, 4, 8, 128), F32), V(tall, F32), V(tall, F32),
            V((32, 8, 128), F32), V((8, 8, 128), F32), V((8, 8, 128), F32), V((32, 8, 128), F32),
            V((8, 48, 128), F32), V((8, 48, 128), F32), V((48, 128), F32), V((32, 1, 128), F32),
            V((1, 128), F32), V((8, 1, 128), F32),
            pltpu.SemaphoreType.DMA((7,)), pltpu.SemaphoreType.DMA((3,)), pltpu.SemaphoreType.DMA((8,)),
            pltpu.SemaphoreType.DMA((8,)), pltpu.SemaphoreType.DMA((3, 4)), pltpu.SemaphoreType.DMA((3, 4)),
        ],
        compiler_params=pltpu.CompilerParams(
            collective_id=0, has_side_effects=True, vmem_limit_bytes=48 * 1024 * 1024
        ),
        name="iteration",
    )(
        face_lists[0, 0], block_pattern[0, 0], multiplicity[0, 0], primal_map[0, 0],
        residual[0, 0], prev_direction[0, 0], solution[0, 0], prev_dot.reshape(1, CASES),
        schur[0, 0], neumann_inverse[0, 0], coarse_basis[0, 0], coarse_inverse,
    )
    return tuple(out[None, None] for out in outs)


def solution(mesh):
    field = P("row", "col", None, None, None)
    return jax.shard_map(
        per_device,
        mesh=mesh,
        in_specs=(
            field, field, field, P(), P("row", "col", None, None), P("row", "col", None), P("row", "col", None, None),
            P("row", "col", None, None, None, None), P("row", "col", None, None, None, None),
            P("row", "col", None, None), P("row", "col", None), P("col", None),
        ),
        out_specs=(field, field, field),
        check_vma=False,
    )
```

```python
import jax
import jax.numpy as jnp
from jax import lax
from jax.experimental import pallas as pl
from jax.experimental.pallas import tpu as pltpu
from jax.sharding import PartitionSpec as P

MESH = pl.DeviceIdType.MESH
F32 = jnp.float32
BF16 = jnp.bfloat16
ROWS, COLS = 8, 32
BLOCKS, DOFS, CASES, SLOTS, PRIMALS = 16, 128, 128, 4, 8
OWNED = 32
COARSE = OWNED * COLS
OPPOSITE = (1, 0, 3, 2)


def split(values):
    high = values.astype(BF16)
    return high, (values - high.astype(F32)).astype(BF16)


def mm(left, right):
    return jnp.dot(left, right, preferred_element_type=F32)


def wide(values):
    return jnp.concatenate(split(values), axis=1)


def iteration(
    faces_h, pattern_h, mult_h, pmap_h, prev_dot_h,
    residual_h, previous_h, solution_h, schur_h, neumann_h, basis_h, inverse_h,
    new_solution, out_res, out_dir,
    faces, pattern, mult, pmap, prev_dot,
    nonface, sigma, place, slot_pat,
    residual, previous, solution, schur, neumann, basis, tiles, inverse,
    scaled, local, schur_hi, schur_lo, lifted, spread, chosen, picker,
    direct, direct_hl, image,
    map_got, near_own, near_got,
    face_basis, got_basis, got_local, got_image,
    a_buf, b_own, b_got, c_buf, e_own, e_got, coarse, v_buf, w_own, w_got,
    load_sem, send_sem, recv_sem, face_send, face_recv,
):
    i = lax.axis_index("row")
    j = lax.axis_index("col")
    z, x = j // 4, lax.rem(j, 4)
    row_id = lambda t: (lax.rem(i + t, ROWS), j)
    col_id = lambda t: (i, lax.rem(j + t, COLS))
    face_id = (row_id(ROWS - 1), row_id(1), col_id(COLS - 1), col_id(1))
    z_at = [lax.rem(z + t, 8) * 4 for t in range(8)]
    x_at = [lax.rem(x + t, 4) for t in range(4)]
    z_far, x_far = (4, 3, 5, 2, 6, 1, 7), (2, 1, 3)
    z_ids = [(i, z_at[t] + x) for t in z_far]
    x_ids = [(i, z * 4 + x_at[t]) for t in x_far]
    hops = lambda t: min(t[0], 8 - t[0]) + min(t[1], 4 - t[1])
    offsets = sorted(((dz, dx) for dz in range(8) for dx in range(4) if dz or dx), key=lambda t: -hops(t))
    col_ids = [(i, z_at[dz] + x_at[dx]) for dz, dx in offsets]
    row_ids = [row_id(t) for t in (4, 5, 3, 6, 2, 7, 1)]

    pairs = (
        (faces_h, faces), (pattern_h, pattern), (mult_h, mult), (pmap_h, pmap),
        (residual_h, residual), (basis_h, basis), (inverse_h, inverse), (neumann_h, neumann),
        (schur_h, schur), (previous_h, previous), (solution_h, solution), (prev_dot_h, prev_dot),
    )
    loads = [pltpu.make_async_copy(source, target, load_sem.at[n]) for n, (source, target) in enumerate(pairs)]
    for n in range(6):
        loads[n].start()

    barrier = pltpu.get_barrier_semaphore()
    for peer in z_ids + x_ids + row_ids:
        pl.semaphore_signal(barrier, inc=1, device_id=peer, device_id_type=MESH)
    loads[7].start()
    loads[6].start()

    def push(source, target, peers, stage):
        for peer in peers:
            pltpu.make_async_remote_copy(
                src_ref=source, dst_ref=target, send_sem=send_sem.at[stage], recv_sem=recv_sem.at[stage],
                device_id=peer, device_id_type=MESH,
            ).start()

    def scatter_row(own, got, stage):
        for t in (4, 5, 3, 6, 2, 7, 1):
            pltpu.make_async_remote_copy(
                src_ref=own.at[lax.rem(i + t, ROWS)], dst_ref=got.at[i],
                send_sem=send_sem.at[stage], recv_sem=recv_sem.at[stage],
                device_id=row_id(t), device_id_type=MESH,
            ).start()

    def await_bytes(buffer, count, sem):
        view = buffer.at[pl.ds(0, count)]
        pltpu.make_async_copy(view, view, sem).wait()

    def send_face(own, got, face, group):
        pltpu.make_async_remote_copy(
            src_ref=own, dst_ref=got.at[OPPOSITE[face]],
            send_sem=face_send.at[group, face], recv_sem=face_recv.at[group, OPPOSITE[face]],
            device_id=face_id[face], device_id_type=MESH,
        ).start()

    for n in (2, 3):
        loads[n].wait()
    weight = lambda b: jnp.where(mult[0, b] == 2, F32(0.5), F32(1.0))
    used = lambda s: jnp.where(faces[s // 4, s % 4] < BLOCKS, F32(1.0), F32(0.0))

    lanes = lax.broadcasted_iota(jnp.int32, (1, 128), 1)
    own_map = jnp.zeros((1, 128), jnp.int32)
    for p in range(PRIMALS):
        own_map = jnp.where(lax.rem(lanes, 8) == p, pmap[0, p], own_map)
    home = x * 8 + z
    map_got[home] = own_map.astype(F32)

    loads[4].wait()
    loads[5].wait()

    both = jnp.zeros((16, 2 * CASES), F32)
    for b in range(0, BLOCKS, 2):
        for n in (b, b + 1):
            scaled[n] = wide(residual[n] * weight(n))
        left = jnp.concatenate(split(basis[:, b * DOFS : (b + 2) * DOFS]), axis=0)
        both = both + mm(left, scaled[pl.ds(b, 2)].reshape(2 * DOFS, 2 * CASES))
    a_buf[home] = both[0:8, 0:CASES] + both[0:8, CASES:] + both[8:16, 0:CASES]

    pl.semaphore_wait(barrier, 17)
    push(map_got.at[home], map_got.at[home], z_ids, 0)
    push(a_buf.at[home], a_buf.at[home], z_ids, 1)
    for n in (8, 9, 10, 11):
        loads[n].start()

    for n in (0, 1):
        loads[n].wait()

    def find_nonface(b, count):
        on_face = faces[0, 0] == b
        for s in range(1, 16):
            on_face = jnp.logical_or(on_face, faces[s // 4, s % 4] == b)
        nonface[b] = jnp.where(on_face, -1, count)
        return count + jnp.where(on_face, 0, 1)

    lax.fori_loop(0, BLOCKS, find_nonface, jnp.int32(0))

    def find_sigma(s, count):
        named = faces[s // 4, s % 4]
        free = named >= BLOCKS
        block = jnp.int32(0)
        for b in range(BLOCKS):
            block = jnp.where(nonface[b] == count, b, block)
        sigma[s] = jnp.where(free, block, named)
        return count + jnp.where(free, 1, 0)

    lax.fori_loop(0, BLOCKS, find_sigma, jnp.int32(0))

    def find_place(b, carry):
        slot = jnp.int32(0)
        for s in range(BLOCKS):
            slot = jnp.where(sigma[s] == b, s, slot)
        place[b] = slot
        return carry

    lax.fori_loop(0, BLOCKS, find_place, 0)

    def find_slot_pat(s, carry):
        for k in range(3):
            slot_pat[s, k] = place[pattern[k, 0, sigma[s]]]
        return carry

    lax.fori_loop(0, BLOCKS, find_slot_pat, 0)

    for b in range(BLOCKS):
        tiles[b] = basis[:, b * DOFS : (b + 1) * DOFS]
    for face in (2, 3, 0, 1):
        for k in range(SLOTS):
            b = sigma[face * 4 + k]
            face_basis[face, k] = tiles[b]

    loads[7].wait()

    def local_row(s, dot):
        b = sigma[s]
        blocks = jnp.concatenate([neumann[b, k] for k in range(3)], axis=1)
        high, low = split(blocks)
        values = jnp.concatenate([scaled[pattern[k, 0, b]] for k in range(3)], axis=0)
        both = mm(high, values)
        row = both[:, 0:CASES] + both[:, CASES:] + mm(low, values[:, 0:CASES])
        row = row * weight(b)
        local[s // 4, lax.rem(s, 4)] = row
        return dot + jnp.sum((residual[b] * row).reshape(16, 8, CASES), axis=0)

    local_dot = lax.fori_loop(0, BLOCKS, local_row, jnp.zeros((8, CASES), F32), unroll=2)
    local_dot = jnp.sum(local_dot, axis=0, keepdims=True)
    line_of = lambda buffer: buffer.at[pl.ds(x * 8, 8)]
    await_bytes(map_got, 7, recv_sem.at[0])
    push(line_of(map_got), line_of(map_got), x_ids, 2)
    await_bytes(a_buf, 7, recv_sem.at[1])
    push(line_of(a_buf), line_of(a_buf), x_ids, 3)
    for face in (2, 3, 0, 1):
        send_face(face_basis.at[face], got_basis, face, 0)

    await_bytes(map_got, 24, recv_sem.at[2])
    group = lanes // 8
    code = jnp.where(lax.rem(lanes, 8) == 0, F32(-1.0), F32(-2.0))
    before, after = lax.rem(j + COLS - 1, COLS), lax.rem(j + 1, COLS)
    west = map_got[lax.rem(before, 4) * 8 + before // 4]
    east = map_got[lax.rem(after, 4) * 8 + after // 4]
    quarter = lax.rem(group, 4)
    near_own[...] = jnp.where(quarter == 0, map_got[home], jnp.where(quarter == 1, west, jnp.where(quarter == 2, east, code)))
    near_got[i] = near_own[...]
    push(near_own, near_got.at[i], row_ids, 4)
    halves = []
    for half in range(2):
        line = jnp.zeros((1, 128), F32)
        for t in range(16):
            line = jnp.where(group == t, map_got[half * 16 + t], line)
        halves.append(line.astype(jnp.int32))
    entries = jnp.concatenate(halves, axis=1)
    loads[6].wait()

    def pick(c, total):
        rows = lax.broadcasted_iota(jnp.int32, (256, 256), 0) + c * 256
        hot = jnp.where(rows == entries, F32(1.0), F32(0.0)).astype(BF16)
        return total + mm(wide_rows(inverse[:, pl.ds(pl.multiple_of(c * 256, 256), 256)]), hot)

    wide_rows = lambda values: jnp.concatenate(split(values), axis=0)
    total = lax.fori_loop(0, COARSE // 256, pick, jnp.zeros((2 * OWNED, 256), F32))
    columns_hi, columns_lo = split(total[0:OWNED] + total[OWNED:])
    rows = lax.broadcasted_iota(jnp.int32, (64, OWNED), 0)
    cols = lax.broadcasted_iota(jnp.int32, (64, OWNED), 1)
    spot = (rows // 8) * 4 + lax.rem(rows, 4)
    first = lax.rem(rows, 8) < 4
    order = jnp.where(jnp.logical_and(first, spot == cols), F32(1.0), F32(0.0)).astype(BF16)
    rows = lax.broadcasted_iota(jnp.int32, (64, 256), 0)
    spot = (rows // 8) * 4 + lax.rem(rows, 4) + j * OWNED
    first = lax.rem(rows, 8) < 4
    own_hot = jnp.where(jnp.logical_and(jnp.logical_not(first), spot == entries), F32(1.0), F32(0.0))
    chosen[0:64] = (mm(order, columns_hi) + own_hot).astype(BF16)
    chosen[64:128] = mm(order, columns_lo).astype(BF16)

    await_bytes(a_buf, 24, recv_sem.at[3])
    both = mm(chosen[...], wide(a_buf[...].reshape(COLS * PRIMALS, CASES)))
    parts = both[0:64, 0:CASES] + both[0:64, CASES:] + both[64:128, 0:CASES]
    b_own[...] = parts.reshape(ROWS, 8, CASES)
    b_got[i] = b_own[i]
    scatter_row(b_own, b_got, 5)

    await_bytes(near_got, ROWS - 1, recv_sem.at[4])
    for half in range(2):
        line = jnp.zeros((1, 128), F32)
        for t in range(4):
            line = jnp.where(lanes // 32 == t, near_got[half * 4 + t], line)
        line = line.astype(jnp.int32)
        here = jnp.logical_and(line >= 0, lax.rem(line // 4, 8) == i)
        where_at = jnp.where(here, (line // OWNED) * 8 + lax.rem(line, 4), -1)
        for quarter_rows in range(2):
            rows = lax.broadcasted_iota(jnp.int32, (128, 128), 0) + quarter_rows * 128
            hit = jnp.logical_or(rows == where_at, jnp.logical_and(line == -1, lax.rem(rows, 8) == 4))
            hot = jnp.where(hit, F32(1.0), F32(0.0))
            picker[pl.ds(half * 128, 128), pl.ds(quarter_rows * 128, 128)] = jnp.transpose(hot).astype(BF16)

    await_bytes(b_got, ROWS - 1, recv_sem.at[5])
    held = jnp.sum(b_got[...], axis=0)
    dot = 0.5 * jnp.sum(held * pltpu.roll(held, 4, 0), axis=0, keepdims=True) + local_dot
    rows = lax.broadcasted_iota(jnp.int32, (8, CASES), 0)
    c_buf[j] = jnp.where(rows < 4, held, jnp.where(rows == 4, jnp.broadcast_to(dot, (8, CASES)), F32(0.0)))
    push(c_buf.at[j], c_buf.at[j], col_ids, 6)
    for face in (2, 3, 0, 1):
        send_face(local.at[face], got_local, face, 1)

    loads[8].wait()

    def order_schur(s, carry):
        b = sigma[s]
        high, low = split(jnp.concatenate([schur[b, k] for k in range(3)], axis=1))
        schur_hi[s] = high
        schur_lo[s] = low
        return carry

    lax.fori_loop(0, BLOCKS, order_schur, 0)

    for face in range(4):
        await_bytes(got_basis.at[face], SLOTS, face_recv.at[0, face])

    def lift(s, carry):
        b = sigma[s]
        own = tiles[b]
        other = got_basis[s // 4, lax.rem(s, 4)] * used(s)
        stack = jnp.concatenate([own, other], axis=0) * weight(b)
        high, low = split(stack)
        high = high.astype(F32)
        full = jnp.concatenate([high, high, low.astype(F32), jnp.zeros((80, DOFS), F32)], axis=0)
        lifted[s] = jnp.transpose(full).astype(BF16)
        return carry

    lax.fori_loop(0, BLOCKS, lift, 0)

    await_bytes(c_buf, COLS - 1, recv_sem.at[6])
    both = mm(picker[...], wide(c_buf[...].reshape(COLS * 8, CASES)))
    spread[...] = (both[:, 0:CASES] + both[:, CASES:]).reshape(ROWS, 32, CASES)
    for t in range(ROWS):
        e_own[t, 0:8] = spread[t, 0:8]
        e_own[t, 8:16] = spread[(t + 7) % ROWS, 0:8]
        e_own[t, 16:24] = spread[(t + 1) % ROWS, 0:8]
        e_own[t, 24:48] = spread[t, 8:32]
    e_got[i] = e_own[i]
    scatter_row(e_own, e_got, 7)
    for face in range(4):
        await_bytes(got_local.at[face], SLOTS, face_recv.at[1, face])
        await_bytes(local.at[face], SLOTS, face_send.at[1, face])

    def add_faces(s, carry):
        local[s // 4, lax.rem(s, 4)] = local[s // 4, lax.rem(s, 4)] + used(s) * got_local[s // 4, lax.rem(s, 4)]
        return carry

    lax.fori_loop(0, BLOCKS, add_faces, 0)
    loads[9].wait()

    await_bytes(e_got, ROWS - 1, recv_sem.at[7])
    loads[11].wait()
    coarse[...] = jnp.sum(e_got[...], axis=0)
    precond_dot = coarse[40:41]
    mix = precond_dot / prev_dot[...]

    for face in range(4):
        stack = jnp.concatenate([coarse[0:8], coarse[8 + 8 * face : 16 + 8 * face]], axis=0)
        high, low = split(stack)
        high = high.astype(F32)
        right = jnp.concatenate([high, low.astype(F32), high, jnp.zeros((80, CASES), F32)], axis=0).astype(BF16)
        for k in range(SLOTS):
            s = face * 4 + k
            value = local[face, k] + mm(lifted[s], right) + mix * previous[sigma[s]]
            direct[s] = value
            direct_hl[s] = wide(value)

    total = jnp.zeros((8, CASES), F32)
    for face in (2, 3, 0, 1):
        def image_row(k, total):
            s = face * 4 + k
            values = jnp.concatenate([direct_hl[slot_pat[s, n]] for n in range(3)], axis=0)
            both = mm(schur_hi[s], values)
            row = both[:, 0:CASES] + both[:, CASES:] + mm(schur_lo[s], values[:, 0:CASES])
            image[face, k] = row
            return total + jnp.sum((direct[s] * row).reshape(16, 8, CASES), axis=0)

        total = lax.fori_loop(0, SLOTS, image_row, total, unroll=2)

    v_buf[j] = jnp.sum(total, axis=0, keepdims=True)
    push(v_buf.at[j], v_buf.at[j], col_ids, 8)
    for face in (2, 3, 0, 1):
        send_face(image.at[face], got_image, face, 2)

    def order_direction(b, carry):
        out_dir[b] = direct[place[b]]
        return carry

    lax.fori_loop(0, BLOCKS, order_direction, 0)
    loads[10].wait()

    await_bytes(v_buf, COLS - 1, recv_sem.at[8])
    w_own[...] = jnp.sum(v_buf[...], axis=0)
    w_got[i] = w_own[...]
    push(w_own, w_got.at[i], row_ids, 9)
    await_bytes(w_got, ROWS - 1, recv_sem.at[9])
    step_size = precond_dot / jnp.sum(w_got[...], axis=0)

    def move(b, carry):
        new_solution[b] = solution[b] + step_size * out_dir[b]
        return carry

    lax.fori_loop(0, BLOCKS, move, 0)

    for face in range(4):
        await_bytes(got_image.at[face], SLOTS, face_recv.at[2, face])

    def finish(b, carry):
        s = place[b]
        full = image[s // 4, lax.rem(s, 4)] + used(s) * got_image[s // 4, lax.rem(s, 4)]
        out_res[b] = residual[b] - step_size * full
        return carry

    lax.fori_loop(0, BLOCKS, finish, 0)

    for buffer, count, stage in (
        (map_got, 7, 0), (a_buf, 7, 1), (map_got, 24, 2), (a_buf, 24, 3), (near_got, 7, 4), (b_got, 7, 5),
        (c_buf, 31, 6), (e_got, 7, 7), (v_buf, 31, 8), (w_got, 7, 9),
    ):
        await_bytes(buffer, count, send_sem.at[stage])
    for face in range(4):
        await_bytes(face_basis.at[face], SLOTS, face_send.at[0, face])
        await_bytes(image.at[face], SLOTS, face_send.at[2, face])


def deliver(a, b, c, a_out, b_out, c_out, sem):
    copies = [pltpu.make_async_copy(s, t, sem.at[n]) for n, (s, t) in enumerate(((a, a_out), (b, b_out), (c, c_out)))]
    for copy in copies:
        copy.start()
    for copy in copies:
        copy.wait()


def per_device(
    solution, residual, prev_direction, prev_dot, face_lists, multiplicity, block_pattern,
    schur, neumann_inverse, coarse_basis, primal_map, coarse_inverse,
):
    field = jax.ShapeDtypeStruct((BLOCKS, DOFS, CASES), F32)
    hbm = pl.BlockSpec(memory_space=pltpu.HBM)
    anywhere = pl.BlockSpec(memory_space=pl.ANY)
    V = pltpu.VMEM
    tall = (4, SLOTS, DOFS, CASES)
    outs = pl.pallas_call(
        iteration,
        out_shape=(pltpu.VMEM((BLOCKS, DOFS, CASES), F32),) * 3,
        in_specs=[hbm] * 12,
        out_specs=(pl.BlockSpec(memory_space=pltpu.VMEM),) * 3,
        scratch_shapes=[
            pltpu.SMEM((4, 4), jnp.int32), pltpu.SMEM((3, 1, 16), jnp.int32), pltpu.SMEM((1, 16), jnp.int32),
            pltpu.SMEM((1, 8), jnp.int32), V((1, 128), F32),
            pltpu.SMEM((16,), jnp.int32), pltpu.SMEM((16,), jnp.int32), pltpu.SMEM((16,), jnp.int32),
            pltpu.SMEM((16, 3), jnp.int32),
            V((16, 128, 128), F32), V((16, 128, 128), F32), V((16, 128, 128), F32),
            V((16, 3, 128, 128), F32), V((16, 3, 128, 128), F32), V((8, 2048), F32), V((16, 8, 128), F32), V((32, 1024), F32),
            V((16, 128, 256), BF16), V(tall, F32), V((16, 128, 384), BF16), V((16, 128, 384), BF16),
            V((16, 128, 128), BF16), V((8, 32, 128), F32), V((128, 256), BF16), V((256, 256), BF16),
            V((16, 128, 128), F32), V((16, 128, 256), BF16), V(tall, F32),
            V((32, 1, 128), F32), V((1, 128), F32), V((8, 1, 128), F32),
            V((4, 4, 8, 128), F32), V((4, 4, 8, 128), F32), V(tall, F32), V(tall, F32),
            V((32, 8, 128), F32), V((8, 8, 128), F32), V((8, 8, 128), F32), V((32, 8, 128), F32),
            V((8, 48, 128), F32), V((8, 48, 128), F32), V((48, 128), F32), V((32, 1, 128), F32),
            V((1, 128), F32), V((8, 1, 128), F32),
            pltpu.SemaphoreType.DMA((12,)), pltpu.SemaphoreType.DMA((10,)),
            pltpu.SemaphoreType.DMA((10,)), pltpu.SemaphoreType.DMA((3, 4)), pltpu.SemaphoreType.DMA((3, 4)),
        ],
        compiler_params=pltpu.CompilerParams(
            collective_id=0, has_side_effects=True, vmem_limit_bytes=48 * 1024 * 1024
        ),
        name="iteration",
    )(*(pltpu.with_memory_space_constraint(value, pltpu.HBM) for value in (
        face_lists[0, 0], jnp.transpose(block_pattern, (0, 3, 1, 2))[0], multiplicity[0], primal_map[0],
        prev_dot.reshape(1, CASES), residual[0, 0], prev_direction[0, 0], solution[0, 0],
        schur[0, 0], neumann_inverse[0, 0], coarse_basis[0, 0], coarse_inverse,
    )))
    outs = pl.pallas_call(
        deliver,
        out_shape=(field, field, field),
        in_specs=[anywhere] * 3,
        out_specs=(hbm, hbm, hbm),
        scratch_shapes=[pltpu.SemaphoreType.DMA((3,))],
        compiler_params=pltpu.CompilerParams(vmem_limit_bytes=1024 * 1024),
        name="deliver",
    )(*outs)
    return tuple(out[None, None] for out in outs)


def solution(mesh):
    field = P("row", "col", None, None, None)
    return jax.shard_map(
        per_device,
        mesh=mesh,
        in_specs=(
            field, field, field, P(), P("row", "col", None, None), P("row", "col", None), P("row", "col", None, None),
            P("row", "col", None, None, None, None), P("row", "col", None, None, None, None),
            P("row", "col", None, None), P("row", "col", None), P("col", None),
        ),
        out_specs=(field, field, field),
        check_vma=False,
    )
```

```python
import jax
import jax.numpy as jnp
from jax import lax
from jax.experimental import pallas as pl
from jax.experimental.pallas import tpu as pltpu
from jax.sharding import PartitionSpec as P

MESH = pl.DeviceIdType.MESH
F32 = jnp.float32
BF16 = jnp.bfloat16
ROWS, COLS = 8, 32
BLOCKS, DOFS, CASES, SLOTS, PRIMALS = 16, 128, 128, 4, 8
CHUNKS = 4
OWNED = 32
COARSE = OWNED * COLS
OPPOSITE = (1, 0, 3, 2)


def split(values):
    high = values.astype(BF16)
    return high, (values - high.astype(F32)).astype(BF16)


def mm(left, right):
    return jnp.dot(left, right, preferred_element_type=F32)


def wide(values):
    return jnp.concatenate(split(values), axis=1)


def tile(values):
    high, low = split(values)
    top = jnp.concatenate([high, low], axis=1)
    return jnp.concatenate([top, jnp.concatenate([high, jnp.zeros_like(low)], axis=1)], axis=0)


def iteration(
    faces_h, pattern_h, mult_h, pmap_h, prev_dot_h,
    residual_h, previous_h, solution_h, schur_h, neumann_h, basis_h, inverse_h,
    solution, residual, out_image, out_dir, step,
    faces, pattern, mult, pmap, prev_dot,
    nonface, sigma, place, slot_pat,
    previous, schur, neumann, basis, tiles, inverse,
    scaled, local, stiff, lifted, spread, chosen, picker,
    direct, tiles_hl, image,
    map_got, near_own, near_got,
    face_basis, got_basis, got_local, got_image,
    a_buf, b_own, b_got, c_buf, e_own, e_got, coarse, v_buf, w_own, w_got,
    load_sem, send_sem, recv_sem, face_send, face_recv,
):
    i = lax.axis_index("row")
    j = lax.axis_index("col")
    z, x = j // 4, lax.rem(j, 4)
    row_id = lambda t: (lax.rem(i + t, ROWS), j)
    col_id = lambda t: (i, lax.rem(j + t, COLS))
    face_id = (row_id(ROWS - 1), row_id(1), col_id(COLS - 1), col_id(1))
    z_at = [lax.rem(z + t, 8) * 4 for t in range(8)]
    x_at = [lax.rem(x + t, 4) for t in range(4)]
    z_far, x_far = (4, 3, 5, 2, 6, 1, 7), (2, 1, 3)
    z_ids = [(i, z_at[t] + x) for t in z_far]
    x_ids = [(i, z * 4 + x_at[t]) for t in x_far]
    hops = lambda t: min(t[0], 8 - t[0]) + min(t[1], 4 - t[1])
    offsets = sorted(((dz, dx) for dz in range(8) for dx in range(4) if dz or dx), key=lambda t: -hops(t))
    col_ids = [(i, z_at[dz] + x_at[dx]) for dz, dx in offsets]
    row_ids = [row_id(t) for t in (4, 5, 3, 6, 2, 7, 1)]

    pairs = (
        (faces_h, faces), (pattern_h, pattern), (mult_h, mult), (pmap_h, pmap),
        (residual_h, residual), (basis_h, basis), (inverse_h, inverse), (neumann_h, neumann),
        (schur_h, schur), (previous_h, previous), (solution_h, solution), (prev_dot_h, prev_dot),
    )
    loads = [pltpu.make_async_copy(source, target, load_sem.at[n]) for n, (source, target) in enumerate(pairs)]
    for n in range(6):
        loads[n].start()

    barrier = pltpu.get_barrier_semaphore()
    for peer in z_ids + x_ids + row_ids:
        pl.semaphore_signal(barrier, inc=1, device_id=peer, device_id_type=MESH)
    loads[7].start()
    loads[6].start()

    def push(source, target, peers, stage):
        for peer in peers:
            pltpu.make_async_remote_copy(
                src_ref=source, dst_ref=target, send_sem=send_sem.at[stage], recv_sem=recv_sem.at[stage],
                device_id=peer, device_id_type=MESH,
            ).start()

    def scatter_row(own, got, stage):
        for t in (4, 5, 3, 6, 2, 7, 1):
            pltpu.make_async_remote_copy(
                src_ref=own.at[lax.rem(i + t, ROWS)], dst_ref=got.at[i],
                send_sem=send_sem.at[stage], recv_sem=recv_sem.at[stage],
                device_id=row_id(t), device_id_type=MESH,
            ).start()

    def await_bytes(buffer, count, sem):
        view = buffer.at[pl.ds(0, count)]
        pltpu.make_async_copy(view, view, sem).wait()

    def send_face(own, got, face, group):
        pltpu.make_async_remote_copy(
            src_ref=own, dst_ref=got.at[OPPOSITE[face]],
            send_sem=face_send.at[group, face], recv_sem=face_recv.at[group, OPPOSITE[face]],
            device_id=face_id[face], device_id_type=MESH,
        ).start()

    for n in (2, 3):
        loads[n].wait()
    weight = lambda b: jnp.where(mult[0, b] == 2, F32(0.5), F32(1.0))
    used = lambda s: jnp.where(faces[s // 4, s % 4] < BLOCKS, F32(1.0), F32(0.0))

    lanes = lax.broadcasted_iota(jnp.int32, (1, 128), 1)
    own_map = jnp.zeros((1, 128), jnp.int32)
    for p in range(PRIMALS):
        own_map = jnp.where(lax.rem(lanes, 8) == p, pmap[0, p], own_map)
    home = x * 8 + z
    map_got[home] = own_map.astype(F32)

    loads[4].wait()
    loads[5].wait()

    both = jnp.zeros((16, 2 * CASES), F32)
    for b in range(0, BLOCKS, 2):
        for n in (b, b + 1):
            scaled[n] = wide(residual[n] * weight(n))
        left = jnp.concatenate(split(basis[:, b * DOFS : (b + 2) * DOFS]), axis=0)
        both = both + mm(left, scaled[pl.ds(b, 2)].reshape(2 * DOFS, 2 * CASES))
    a_buf[home] = both[0:8, 0:CASES] + both[0:8, CASES:] + both[8:16, 0:CASES]

    pl.semaphore_wait(barrier, 17)
    push(map_got.at[home], map_got.at[home], z_ids, 0)
    push(a_buf.at[home], a_buf.at[home], z_ids, 1)
    for n in (8, 9, 10, 11):
        loads[n].start()

    for n in (0, 1):
        loads[n].wait()

    def find_nonface(b, count):
        on_face = faces[0, 0] == b
        for s in range(1, 16):
            on_face = jnp.logical_or(on_face, faces[s // 4, s % 4] == b)
        nonface[b] = jnp.where(on_face, -1, count)
        return count + jnp.where(on_face, 0, 1)

    lax.fori_loop(0, BLOCKS, find_nonface, jnp.int32(0))

    def find_sigma(s, count):
        named = faces[s // 4, s % 4]
        free = named >= BLOCKS
        block = jnp.int32(0)
        for b in range(BLOCKS):
            block = jnp.where(nonface[b] == count, b, block)
        sigma[s] = jnp.where(free, block, named)
        return count + jnp.where(free, 1, 0)

    lax.fori_loop(0, BLOCKS, find_sigma, jnp.int32(0))

    def find_place(b, carry):
        slot = jnp.int32(0)
        for s in range(BLOCKS):
            slot = jnp.where(sigma[s] == b, s, slot)
        place[b] = slot
        return carry

    lax.fori_loop(0, BLOCKS, find_place, 0)

    def find_slot_pat(s, carry):
        for k in range(3):
            slot_pat[s, k] = place[pattern[k, 0, sigma[s]]]
        return carry

    lax.fori_loop(0, BLOCKS, find_slot_pat, 0)

    for b in range(BLOCKS):
        tiles[b] = basis[:, b * DOFS : (b + 1) * DOFS]
    for face in (2, 3, 0, 1):
        for k in range(SLOTS):
            b = sigma[face * 4 + k]
            face_basis[face, k] = tiles[b]

    loads[7].wait()

    def local_row(s, dot):
        b = sigma[s]
        blocks = jnp.concatenate([neumann[b, k] for k in range(3)], axis=1)
        high, low = split(blocks)
        values = jnp.concatenate([scaled[pattern[k, 0, b]] for k in range(3)], axis=0)
        both = mm(high, values)
        row = both[:, 0:CASES] + both[:, CASES:] + mm(low, values[:, 0:CASES])
        row = row * weight(b)
        local[s // 4, lax.rem(s, 4)] = row
        return dot + jnp.sum((residual[b] * row).reshape(16, 8, CASES), axis=0)

    local_dot = lax.fori_loop(0, BLOCKS, local_row, jnp.zeros((8, CASES), F32), unroll=2)
    local_dot = jnp.sum(local_dot, axis=0, keepdims=True)
    line_of = lambda buffer: buffer.at[pl.ds(x * 8, 8)]
    await_bytes(map_got, 7, recv_sem.at[0])
    push(line_of(map_got), line_of(map_got), x_ids, 2)
    await_bytes(a_buf, 7, recv_sem.at[1])
    push(line_of(a_buf), line_of(a_buf), x_ids, 3)
    for face in (2, 3, 0, 1):
        send_face(face_basis.at[face], got_basis, face, 0)

    await_bytes(map_got, 24, recv_sem.at[2])
    group = lanes // 8
    code = jnp.where(lax.rem(lanes, 8) == 0, F32(-1.0), F32(-2.0))
    before, after = lax.rem(j + COLS - 1, COLS), lax.rem(j + 1, COLS)
    west = map_got[lax.rem(before, 4) * 8 + before // 4]
    east = map_got[lax.rem(after, 4) * 8 + after // 4]
    quarter = lax.rem(group, 4)
    near_own[...] = jnp.where(quarter == 0, map_got[home], jnp.where(quarter == 1, west, jnp.where(quarter == 2, east, code)))
    near_got[i] = near_own[...]
    push(near_own, near_got.at[i], row_ids, 4)
    halves = []
    for half in range(2):
        line = jnp.zeros((1, 128), F32)
        for t in range(16):
            line = jnp.where(group == t, map_got[half * 16 + t], line)
        halves.append(line.astype(jnp.int32))
    entries = jnp.concatenate(halves, axis=1)
    loads[6].wait()

    def pick(c, total):
        rows = lax.broadcasted_iota(jnp.int32, (256, 256), 0) + c * 256
        hot = jnp.where(rows == entries, F32(1.0), F32(0.0)).astype(BF16)
        return total + mm(wide_rows(inverse[:, pl.ds(pl.multiple_of(c * 256, 256), 256)]), hot)

    wide_rows = lambda values: jnp.concatenate(split(values), axis=0)
    total = lax.fori_loop(0, COARSE // 256, pick, jnp.zeros((2 * OWNED, 256), F32))
    columns_hi, columns_lo = split(total[0:OWNED] + total[OWNED:])
    rows = lax.broadcasted_iota(jnp.int32, (64, OWNED), 0)
    cols = lax.broadcasted_iota(jnp.int32, (64, OWNED), 1)
    spot = (rows // 8) * 4 + lax.rem(rows, 4)
    first = lax.rem(rows, 8) < 4
    order = jnp.where(jnp.logical_and(first, spot == cols), F32(1.0), F32(0.0)).astype(BF16)
    rows = lax.broadcasted_iota(jnp.int32, (64, 256), 0)
    spot = (rows // 8) * 4 + lax.rem(rows, 4) + j * OWNED
    first = lax.rem(rows, 8) < 4
    own_hot = jnp.where(jnp.logical_and(jnp.logical_not(first), spot == entries), F32(1.0), F32(0.0))
    chosen[0:64] = (mm(order, columns_hi) + own_hot).astype(BF16)
    chosen[64:128] = mm(order, columns_lo).astype(BF16)

    await_bytes(a_buf, 24, recv_sem.at[3])
    both = mm(chosen[...], wide(a_buf[...].reshape(COLS * PRIMALS, CASES)))
    parts = both[0:64, 0:CASES] + both[0:64, CASES:] + both[64:128, 0:CASES]
    b_own[...] = parts.reshape(ROWS, 8, CASES)
    b_got[i] = b_own[i]
    scatter_row(b_own, b_got, 5)

    await_bytes(near_got, ROWS - 1, recv_sem.at[4])
    for half in range(2):
        line = jnp.zeros((1, 128), F32)
        for t in range(4):
            line = jnp.where(lanes // 32 == t, near_got[half * 4 + t], line)
        line = line.astype(jnp.int32)
        here = jnp.logical_and(line >= 0, lax.rem(line // 4, 8) == i)
        where_at = jnp.where(here, (line // OWNED) * 8 + lax.rem(line, 4), -1)
        for quarter_rows in range(2):
            rows = lax.broadcasted_iota(jnp.int32, (128, 128), 0) + quarter_rows * 128
            hit = jnp.logical_or(rows == where_at, jnp.logical_and(line == -1, lax.rem(rows, 8) == 4))
            hot = jnp.where(hit, F32(1.0), F32(0.0))
            picker[pl.ds(half * 128, 128), pl.ds(quarter_rows * 128, 128)] = jnp.transpose(hot).astype(BF16)

    await_bytes(b_got, ROWS - 1, recv_sem.at[5])
    held = jnp.sum(b_got[...], axis=0)
    dot = 0.5 * jnp.sum(held * pltpu.roll(held, 4, 0), axis=0, keepdims=True) + local_dot
    rows = lax.broadcasted_iota(jnp.int32, (8, CASES), 0)
    c_buf[j] = jnp.where(rows < 4, held, jnp.where(rows == 4, jnp.broadcast_to(dot, (8, CASES)), F32(0.0)))
    push(c_buf.at[j], c_buf.at[j], col_ids, 6)
    for face in (2, 3, 0, 1):
        send_face(local.at[face], got_local, face, 1)

    loads[8].wait()

    def order_schur(s, carry):
        b = sigma[s]
        for k in range(3):
            stiff[s, :, 2 * k * DOFS : 2 * (k + 1) * DOFS] = wide(schur[b, k])
        return carry

    lax.fori_loop(0, BLOCKS, order_schur, 0)

    for face in range(4):
        await_bytes(got_basis.at[face], SLOTS, face_recv.at[0, face])

    def lift(s, carry):
        b = sigma[s]
        own = tiles[b]
        other = got_basis[s // 4, lax.rem(s, 4)] * used(s)
        stack = jnp.concatenate([own, other], axis=0) * weight(b)
        high, low = split(stack)
        high = high.astype(F32)
        full = jnp.concatenate([high, high, low.astype(F32), jnp.zeros((80, DOFS), F32)], axis=0)
        lifted[s] = jnp.transpose(full).astype(BF16)
        return carry

    lax.fori_loop(0, BLOCKS, lift, 0)

    await_bytes(c_buf, COLS - 1, recv_sem.at[6])
    both = mm(picker[...], wide(c_buf[...].reshape(COLS * 8, CASES)))
    spread[...] = (both[:, 0:CASES] + both[:, CASES:]).reshape(ROWS, 32, CASES)
    for t in range(ROWS):
        e_own[t, 0:8] = spread[t, 0:8]
        e_own[t, 8:16] = spread[(t + 7) % ROWS, 0:8]
        e_own[t, 16:24] = spread[(t + 1) % ROWS, 0:8]
        e_own[t, 24:48] = spread[t, 8:32]
    e_got[i] = e_own[i]
    scatter_row(e_own, e_got, 7)
    for face in range(4):
        await_bytes(got_local.at[face], SLOTS, face_recv.at[1, face])
        await_bytes(local.at[face], SLOTS, face_send.at[1, face])

    def add_faces(s, carry):
        local[s // 4, lax.rem(s, 4)] = local[s // 4, lax.rem(s, 4)] + used(s) * got_local[s // 4, lax.rem(s, 4)]
        return carry

    lax.fori_loop(0, BLOCKS, add_faces, 0)
    loads[9].wait()

    await_bytes(e_got, ROWS - 1, recv_sem.at[7])
    loads[11].wait()
    coarse[...] = jnp.sum(e_got[...], axis=0)
    precond_dot = coarse[40:41]
    mix = precond_dot / prev_dot[...]

    for face in range(4):
        stack = jnp.concatenate([coarse[0:8], coarse[8 + 8 * face : 16 + 8 * face]], axis=0)
        high, low = split(stack)
        high = high.astype(F32)
        right = jnp.concatenate([high, low.astype(F32), high, jnp.zeros((80, CASES), F32)], axis=0).astype(BF16)
        for k in range(SLOTS):
            s = face * 4 + k
            value = local[face, k] + mm(lifted[s], right) + mix * previous[sigma[s]]
            direct[s] = value
            tiles_hl[s] = tile(value)

    total = jnp.zeros((8, CASES), F32)
    for face in (2, 3, 0, 1):
        def image_row(k, total):
            s = face * 4 + k
            both = mm(stiff[s, :, 0:256], tiles_hl[slot_pat[s, 0]])
            both = both + mm(stiff[s, :, 256:512], tiles_hl[slot_pat[s, 1]])
            both = both + mm(stiff[s, :, 512:768], tiles_hl[slot_pat[s, 2]])
            row = both[:, 0:CASES] + both[:, CASES:]
            image[face, k] = row
            return total + jnp.sum((direct[s] * row).reshape(16, 8, CASES), axis=0)

        total = lax.fori_loop(0, SLOTS, image_row, total, unroll=True)

    v_buf[j] = jnp.sum(total, axis=0, keepdims=True)
    push(v_buf.at[j], v_buf.at[j], col_ids, 8)
    for face in (2, 3, 0, 1):
        send_face(image.at[face], got_image, face, 2)

    def order_direction(b, carry):
        out_dir[b] = direct[place[b]]
        return carry

    lax.fori_loop(0, BLOCKS, order_direction, 0)
    loads[10].wait()

    await_bytes(v_buf, COLS - 1, recv_sem.at[8])
    w_own[...] = jnp.sum(v_buf[...], axis=0)
    w_got[i] = w_own[...]
    push(w_own, w_got.at[i], row_ids, 9)

    for face in range(4):
        await_bytes(got_image.at[face], SLOTS, face_recv.at[2, face])

    def order_image(b, carry):
        s = place[b]
        out_image[b] = image[s // 4, lax.rem(s, 4)] + used(s) * got_image[s // 4, lax.rem(s, 4)]
        return carry

    lax.fori_loop(0, BLOCKS, order_image, 0)

    await_bytes(w_got, ROWS - 1, recv_sem.at[9])
    step[...] = precond_dot / jnp.sum(w_got[...], axis=0)

    for buffer, count, stage in (
        (map_got, 7, 0), (a_buf, 7, 1), (map_got, 24, 2), (a_buf, 24, 3), (near_got, 7, 4), (b_got, 7, 5),
        (c_buf, 31, 6), (e_got, 7, 7), (v_buf, 31, 8), (w_got, 7, 9),
    ):
        await_bytes(buffer, count, send_sem.at[stage])
    for face in range(4):
        await_bytes(face_basis.at[face], SLOTS, face_send.at[0, face])
        await_bytes(image.at[face], SLOTS, face_send.at[2, face])


def deliver(
    solution, residual, image, direction, step, new_solution, new_residual, new_direction,
    moved, left, sem,
):
    copies = [pltpu.make_async_copy(direction, new_direction, sem.at[0, 0])]
    copies[0].start()
    step_rows = jnp.broadcast_to(step[...], (DOFS, CASES))
    for part in range(CHUNKS):
        blocks = pl.ds(part * (BLOCKS // CHUNKS), BLOCKS // CHUNKS)
        for b in range(part * (BLOCKS // CHUNKS), (part + 1) * (BLOCKS // CHUNKS)):
            moved[b] = solution[b] + step_rows * direction[b]
            left[b] = residual[b] - step_rows * image[b]
        for n, (source, target) in enumerate(((moved, new_solution), (left, new_residual))):
            copies.append(pltpu.make_async_copy(source.at[blocks], target.at[blocks], sem.at[n + 1, part]))
            copies[-1].start()
    for copy in copies:
        copy.wait()


def per_device(
    solution, residual, prev_direction, prev_dot, face_lists, multiplicity, block_pattern,
    schur, neumann_inverse, coarse_basis, primal_map, coarse_inverse,
):
    field = jax.ShapeDtypeStruct((BLOCKS, DOFS, CASES), F32)
    hbm = pl.BlockSpec(memory_space=pltpu.HBM)
    vmem = pl.BlockSpec(memory_space=pltpu.VMEM)
    V = pltpu.VMEM
    tall = (4, SLOTS, DOFS, CASES)
    outs = pl.pallas_call(
        iteration,
        out_shape=(pltpu.VMEM((BLOCKS, DOFS, CASES), F32),) * 4 + (pltpu.VMEM((1, CASES), F32),),
        in_specs=[hbm] * 12,
        out_specs=(vmem,) * 5,
        scratch_shapes=[
            pltpu.SMEM((4, 4), jnp.int32), pltpu.SMEM((3, 1, 16), jnp.int32), pltpu.SMEM((1, 16), jnp.int32),
            pltpu.SMEM((1, 8), jnp.int32), V((1, 128), F32),
            pltpu.SMEM((16,), jnp.int32), pltpu.SMEM((16,), jnp.int32), pltpu.SMEM((16,), jnp.int32),
            pltpu.SMEM((16, 3), jnp.int32),
            V((16, 128, 128), F32),
            V((16, 3, 128, 128), F32), V((16, 3, 128, 128), F32), V((8, 2048), F32), V((16, 8, 128), F32), V((32, 1024), F32),
            V((16, 128, 256), BF16), V(tall, F32), V((16, 128, 768), BF16),
            V((16, 128, 128), BF16), V((8, 32, 128), F32), V((128, 256), BF16), V((256, 256), BF16),
            V((16, 128, 128), F32), V((16, 256, 256), BF16), V(tall, F32),
            V((32, 1, 128), F32), V((1, 128), F32), V((8, 1, 128), F32),
            V((4, 4, 8, 128), F32), V((4, 4, 8, 128), F32), V(tall, F32), V(tall, F32),
            V((32, 8, 128), F32), V((8, 8, 128), F32), V((8, 8, 128), F32), V((32, 8, 128), F32),
            V((8, 48, 128), F32), V((8, 48, 128), F32), V((48, 128), F32), V((32, 1, 128), F32),
            V((1, 128), F32), V((8, 1, 128), F32),
            pltpu.SemaphoreType.DMA((12,)), pltpu.SemaphoreType.DMA((10,)),
            pltpu.SemaphoreType.DMA((10,)), pltpu.SemaphoreType.DMA((3, 4)), pltpu.SemaphoreType.DMA((3, 4)),
        ],
        compiler_params=pltpu.CompilerParams(
            collective_id=0, has_side_effects=True, vmem_limit_bytes=48 * 1024 * 1024
        ),
        name="iteration",
    )(*(pltpu.with_memory_space_constraint(value, pltpu.HBM) for value in (
        face_lists[0, 0], jnp.transpose(block_pattern, (0, 3, 1, 2))[0], multiplicity[0], primal_map[0],
        prev_dot.reshape(1, CASES), residual[0, 0], prev_direction[0, 0], solution[0, 0],
        schur[0, 0], neumann_inverse[0, 0], coarse_basis[0, 0], coarse_inverse,
    )))
    outs = pl.pallas_call(
        deliver,
        out_shape=(field, field, field),
        in_specs=[vmem] * 5,
        out_specs=(hbm, hbm, hbm),
        scratch_shapes=[
            pltpu.VMEM((BLOCKS, DOFS, CASES), F32), pltpu.VMEM((BLOCKS, DOFS, CASES), F32),
            pltpu.SemaphoreType.DMA((3, CHUNKS)),
        ],
        compiler_params=pltpu.CompilerParams(vmem_limit_bytes=4 * 1024 * 1024),
        name="deliver",
    )(*outs)
    return tuple(out[None, None] for out in outs)


def solution(mesh):
    field = P("row", "col", None, None, None)
    return jax.shard_map(
        per_device,
        mesh=mesh,
        in_specs=(
            field, field, field, P(), P("row", "col", None, None), P("row", "col", None), P("row", "col", None, None),
            P("row", "col", None, None, None, None), P("row", "col", None, None, None, None),
            P("row", "col", None, None), P("row", "col", None), P("col", None),
        ),
        out_specs=(field, field, field),
        check_vma=False,
    )
```

```python
import jax
import jax.numpy as jnp
from jax import lax
from jax.experimental import pallas as pl
from jax.experimental.pallas import tpu as pltpu
from jax.sharding import PartitionSpec as P

MESH = pl.DeviceIdType.MESH
F32 = jnp.float32
BF16 = jnp.bfloat16
ROWS, COLS = 8, 32
BLOCKS, DOFS, CASES, SLOTS, PRIMALS = 16, 128, 128, 4, 8
CHUNKS = 4
OWNED = 32
COARSE = OWNED * COLS
OPPOSITE = (1, 0, 3, 2)


def split(values):
    high = values.astype(BF16)
    return high, (values - high.astype(F32)).astype(BF16)


def mm(left, right):
    return jnp.dot(left, right, preferred_element_type=F32)


def wide(values):
    return jnp.concatenate(split(values), axis=1)


def tile(values):
    high, low = split(values)
    top = jnp.concatenate([high, low], axis=1)
    return jnp.concatenate([top, jnp.concatenate([high, jnp.zeros_like(low)], axis=1)], axis=0)


def iteration(
    faces_h, pattern_h, mult_h, pmap_h, prev_dot_h,
    residual_h, previous_h, solution_h, schur_h, neumann_h, basis_h, inverse_h,
    solution, residual, out_image, out_dir, step,
    faces, pattern, mult, pmap, prev_dot,
    nonface, sigma, place, slot_pat,
    previous, schur, neumann, basis, tiles, inverse,
    scaled, local, stiff, lifted, chosen, picker,
    direct, tiles_hl, image,
    map_got, near_own, near_got,
    face_basis, got_basis, got_local, got_image,
    a_buf, b_own, b_got, c_buf, e_own, e_got, coarse, v_buf, w_own, w_got,
    load_sem, part_sem, send_sem, recv_sem, face_send, face_recv,
):
    i = lax.axis_index("row")
    j = lax.axis_index("col")
    z, x = j // 4, lax.rem(j, 4)
    row_id = lambda t: (lax.rem(i + t, ROWS), j)
    col_id = lambda t: (i, lax.rem(j + t, COLS))
    face_id = (row_id(ROWS - 1), row_id(1), col_id(COLS - 1), col_id(1))
    z_at = [lax.rem(z + t, 8) * 4 for t in range(8)]
    x_at = [lax.rem(x + t, 4) for t in range(4)]
    z_far, x_far = (4, 3, 5, 2, 6, 1, 7), (2, 1, 3)
    z_ids = [(i, z_at[t] + x) for t in z_far]
    x_ids = [(i, z * 4 + x_at[t]) for t in x_far]
    hops = lambda t: min(t[0], 8 - t[0]) + min(t[1], 4 - t[1])
    offsets = sorted(((dz, dx) for dz in range(8) for dx in range(4) if dz or dx), key=lambda t: -hops(t))
    col_ids = [(i, z_at[dz] + x_at[dx]) for dz, dx in offsets]
    row_ids = [row_id(t) for t in (4, 5, 3, 6, 2, 7, 1)]

    pairs = (
        (faces_h, faces), (pattern_h, pattern), (mult_h, mult), (pmap_h, pmap),
        (residual_h, residual), (basis_h, basis), (inverse_h, inverse), (neumann_h, neumann),
        (schur_h, schur), (previous_h, previous), (solution_h, solution), (prev_dot_h, prev_dot),
    )
    loads = [pltpu.make_async_copy(source, target, load_sem.at[n]) for n, (source, target) in enumerate(pairs)]
    parts = [
        pltpu.make_async_copy(residual_h.at[pl.ds(4 * n, 4)], residual.at[pl.ds(4 * n, 4)], part_sem.at[n]) for n in range(4)
    ]
    loads[5].start()
    parts[0].start()
    loads[2].start()
    for n in range(1, 4):
        parts[n].start()
    for n in (3, 0, 1):
        loads[n].start()

    barrier = pltpu.get_barrier_semaphore()
    for peer in z_ids + x_ids + row_ids:
        pl.semaphore_signal(barrier, inc=1, device_id=peer, device_id_type=MESH)
    loads[7].start()
    loads[6].start()

    def push(source, target, peers, stage):
        for peer in peers:
            pltpu.make_async_remote_copy(
                src_ref=source, dst_ref=target, send_sem=send_sem.at[stage], recv_sem=recv_sem.at[stage],
                device_id=peer, device_id_type=MESH,
            ).start()

    def scatter_row(own, got, stage):
        for t in (4, 5, 3, 6, 2, 7, 1):
            pltpu.make_async_remote_copy(
                src_ref=own.at[lax.rem(i + t, ROWS)], dst_ref=got.at[i],
                send_sem=send_sem.at[stage], recv_sem=recv_sem.at[stage],
                device_id=row_id(t), device_id_type=MESH,
            ).start()

    def await_bytes(buffer, count, sem):
        view = buffer.at[pl.ds(0, count)]
        pltpu.make_async_copy(view, view, sem).wait()

    def send_face(own, got, face, group):
        pltpu.make_async_remote_copy(
            src_ref=own, dst_ref=got.at[OPPOSITE[face]],
            send_sem=face_send.at[group, face], recv_sem=face_recv.at[group, OPPOSITE[face]],
            device_id=face_id[face], device_id_type=MESH,
        ).start()

    loads[2].wait()
    weight = lambda b: jnp.where(mult[0, b] == 2, F32(0.5), F32(1.0))
    used = lambda s: jnp.where(faces[s // 4, s % 4] < BLOCKS, F32(1.0), F32(0.0))

    lanes = lax.broadcasted_iota(jnp.int32, (1, 128), 1)
    home = x * 8 + z

    loads[5].wait()

    both = jnp.zeros((16, 2 * CASES), F32)
    for b in range(0, BLOCKS, 2):
        if b % 4 == 0:
            parts[b // 4].wait()
        for n in (b, b + 1):
            scaled[n] = wide(residual[n] * weight(n))
        left = jnp.concatenate(split(basis[:, b * DOFS : (b + 2) * DOFS]), axis=0)
        both = both + mm(left, scaled[pl.ds(b, 2)].reshape(2 * DOFS, 2 * CASES))
    a_buf[home] = both[0:8, 0:CASES] + both[0:8, CASES:] + both[8:16, 0:CASES]

    loads[3].wait()
    own_map = jnp.zeros((1, 128), jnp.int32)
    for p in range(PRIMALS):
        own_map = jnp.where(lax.rem(lanes, 8) == p, pmap[0, p], own_map)
    map_got[home] = own_map.astype(F32)
    pl.semaphore_wait(barrier, 17)
    push(map_got.at[home], map_got.at[home], z_ids, 0)
    push(a_buf.at[home], a_buf.at[home], z_ids, 1)
    for n in (8, 9, 10, 11):
        loads[n].start()

    for n in (0, 1):
        loads[n].wait()

    def send_part(face, first, count):
        part = pl.ds(first, count)
        pltpu.make_async_remote_copy(
            src_ref=image.at[face, part], dst_ref=got_image.at[OPPOSITE[face], part],
            send_sem=face_send.at[2, face], recv_sem=face_recv.at[2, OPPOSITE[face]],
            device_id=face_id[face], device_id_type=MESH,
        ).start()

    def find_nonface(b, count):
        on_face = faces[0, 0] == b
        for s in range(1, 16):
            on_face = jnp.logical_or(on_face, faces[s // 4, s % 4] == b)
        nonface[b] = jnp.where(on_face, -1, count)
        return count + jnp.where(on_face, 0, 1)

    lax.fori_loop(0, BLOCKS, find_nonface, jnp.int32(0))

    def find_sigma(s, count):
        named = faces[s // 4, s % 4]
        free = named >= BLOCKS
        block = jnp.int32(0)
        for b in range(BLOCKS):
            block = jnp.where(nonface[b] == count, b, block)
        sigma[s] = jnp.where(free, block, named)
        return count + jnp.where(free, 1, 0)

    lax.fori_loop(0, BLOCKS, find_sigma, jnp.int32(0))

    def find_place(b, carry):
        slot = jnp.int32(0)
        for s in range(BLOCKS):
            slot = jnp.where(sigma[s] == b, s, slot)
        place[b] = slot
        return carry

    lax.fori_loop(0, BLOCKS, find_place, 0)

    def find_slot_pat(s, carry):
        for k in range(3):
            slot_pat[s, k] = place[pattern[k, 0, sigma[s]]]
        return carry

    lax.fori_loop(0, BLOCKS, find_slot_pat, 0)

    for b in range(BLOCKS):
        tiles[b] = basis[:, b * DOFS : (b + 1) * DOFS]
    for face in (2, 3, 0, 1):
        for k in range(SLOTS):
            b = sigma[face * 4 + k]
            face_basis[face, k] = tiles[b]

    loads[7].wait()

    def local_row(s, dot):
        b = sigma[s]
        blocks = jnp.concatenate([neumann[b, k] for k in range(3)], axis=1)
        high, low = split(blocks)
        values = jnp.concatenate([scaled[pattern[k, 0, b]] for k in range(3)], axis=0)
        both = mm(high, values)
        row = both[:, 0:CASES] + both[:, CASES:] + mm(low, values[:, 0:CASES])
        row = row * weight(b)
        local[s // 4, lax.rem(s, 4)] = row
        return dot + jnp.sum((residual[b] * row).reshape(16, 8, CASES), axis=0)

    local_dot = lax.fori_loop(0, BLOCKS, local_row, jnp.zeros((8, CASES), F32), unroll=2)
    local_dot = jnp.sum(local_dot, axis=0, keepdims=True)
    line_of = lambda buffer: buffer.at[pl.ds(x * 8, 8)]
    await_bytes(map_got, 7, recv_sem.at[0])
    push(line_of(map_got), line_of(map_got), x_ids, 2)
    await_bytes(a_buf, 7, recv_sem.at[1])
    push(line_of(a_buf), line_of(a_buf), x_ids, 3)
    for face in (2, 3, 0, 1):
        send_face(face_basis.at[face], got_basis, face, 0)

    await_bytes(map_got, 24, recv_sem.at[2])
    group = lanes // 8
    code = jnp.where(lax.rem(lanes, 8) == 0, F32(-1.0), F32(-2.0))
    before, after = lax.rem(j + COLS - 1, COLS), lax.rem(j + 1, COLS)
    west = map_got[lax.rem(before, 4) * 8 + before // 4]
    east = map_got[lax.rem(after, 4) * 8 + after // 4]
    quarter = lax.rem(group, 4)
    near_own[...] = jnp.where(quarter == 0, map_got[home], jnp.where(quarter == 1, west, jnp.where(quarter == 2, east, code)))
    near_got[i] = near_own[...]
    push(near_own, near_got.at[i], row_ids, 4)
    halves = []
    for half in range(2):
        line = jnp.zeros((1, 128), F32)
        for t in range(16):
            line = jnp.where(group == t, map_got[half * 16 + t], line)
        halves.append(line.astype(jnp.int32))
    entries = jnp.concatenate(halves, axis=1)
    loads[6].wait()

    def pick(c, total):
        rows = lax.broadcasted_iota(jnp.int32, (256, 256), 0) + c * 256
        hot = jnp.where(rows == entries, F32(1.0), F32(0.0)).astype(BF16)
        return total + mm(wide_rows(inverse[:, pl.ds(pl.multiple_of(c * 256, 256), 256)]), hot)

    wide_rows = lambda values: jnp.concatenate(split(values), axis=0)
    total = lax.fori_loop(0, COARSE // 256, pick, jnp.zeros((2 * OWNED, 256), F32))
    columns_hi, columns_lo = split(total[0:OWNED] + total[OWNED:])
    rows = lax.broadcasted_iota(jnp.int32, (64, OWNED), 0)
    cols = lax.broadcasted_iota(jnp.int32, (64, OWNED), 1)
    spot = (rows // 8) * 4 + lax.rem(rows, 4)
    first = lax.rem(rows, 8) < 4
    order = jnp.where(jnp.logical_and(first, spot == cols), F32(1.0), F32(0.0)).astype(BF16)
    rows = lax.broadcasted_iota(jnp.int32, (64, 256), 0)
    spot = (rows // 8) * 4 + lax.rem(rows, 4) + j * OWNED
    first = lax.rem(rows, 8) < 4
    own_hot = jnp.where(jnp.logical_and(jnp.logical_not(first), spot == entries), F32(1.0), F32(0.0))
    chosen[0:64] = (mm(order, columns_hi) + own_hot).astype(BF16)
    chosen[64:128] = mm(order, columns_lo).astype(BF16)

    await_bytes(a_buf, 24, recv_sem.at[3])
    both = mm(chosen[...], wide(a_buf[...].reshape(COLS * PRIMALS, CASES)))
    parts = both[0:64, 0:CASES] + both[0:64, CASES:] + both[64:128, 0:CASES]
    b_own[...] = parts.reshape(ROWS, 8, CASES)
    b_got[i] = b_own[i]
    scatter_row(b_own, b_got, 5)

    await_bytes(near_got, ROWS - 1, recv_sem.at[4])
    for half in range(2):
        line = jnp.zeros((1, 128), F32)
        for t in range(4):
            line = jnp.where(lanes // 32 == t, near_got[half * 4 + t], line)
        line = line.astype(jnp.int32)
        here = jnp.logical_and(line >= 0, lax.rem(line // 4, 8) == i)
        where_at = jnp.where(here, lax.rem(line, 4) * COLS + line // OWNED, -1)
        for quarter_rows in range(2):
            rows = lax.broadcasted_iota(jnp.int32, (128, 128), 0) + quarter_rows * 128
            hit = jnp.logical_or(rows == where_at, jnp.logical_and(line == -1, rows // COLS == 4))
            hot = jnp.where(hit, F32(1.0), F32(0.0))
            picker[pl.ds(half * 128, 128), pl.ds(quarter_rows * 128, 128)] = jnp.transpose(hot).astype(BF16)

    await_bytes(b_got, ROWS - 1, recv_sem.at[5])
    held = jnp.sum(b_got[...], axis=0)
    dot = 0.5 * jnp.sum(held * pltpu.roll(held, 4, 0), axis=0, keepdims=True) + local_dot
    for q in range(4):
        c_buf[j, :, q * CASES : (q + 1) * CASES] = held[q : q + 1]
    c_buf[j, :, 4 * CASES :] = dot
    push(c_buf.at[j], c_buf.at[j], col_ids, 6)
    for face in (2, 3, 0, 1):
        send_face(local.at[face], got_local, face, 1)

    loads[8].wait()

    def order_schur(s, carry):
        b = sigma[s]
        for k in range(3):
            stiff[s, :, 2 * k * DOFS : 2 * (k + 1) * DOFS] = wide(schur[b, k])
        return carry

    lax.fori_loop(0, BLOCKS, order_schur, 0)

    for face in range(4):
        await_bytes(got_basis.at[face], SLOTS, face_recv.at[0, face])

    def lift(s, carry):
        b = sigma[s]
        own = tiles[b]
        other = got_basis[s // 4, lax.rem(s, 4)] * used(s)
        stack = jnp.concatenate([own, other], axis=0) * weight(b)
        high, low = split(stack)
        high = high.astype(F32)
        full = jnp.concatenate([high, high, low.astype(F32), jnp.zeros((80, DOFS), F32)], axis=0)
        lifted[s] = jnp.transpose(full).astype(BF16)
        return carry

    lax.fori_loop(0, BLOCKS, lift, 0)

    await_bytes(c_buf, COLS - 1, recv_sem.at[6])
    rows_held = [c_buf[:, :, q * CASES : (q + 1) * CASES].reshape(COLS, CASES) for q in range(5)]
    both = mm(picker[...], wide(jnp.concatenate(rows_held + [jnp.zeros((96, CASES), F32)], axis=0)))
    rows_for = both[:, 0:CASES] + both[:, CASES:]
    for t in range(ROWS):
        north, south = (t + 7) % ROWS * 32, (t + 1) % ROWS * 32
        e_own[t, 0:8] = rows_for[t * 32 : t * 32 + 8]
        e_own[t, 8:16] = rows_for[north : north + 8]
        e_own[t, 16:24] = rows_for[south : south + 8]
        e_own[t, 24:48] = rows_for[t * 32 + 8 : t * 32 + 32]
    e_got[i] = e_own[i]
    scatter_row(e_own, e_got, 7)
    for face in range(4):
        await_bytes(got_local.at[face], SLOTS, face_recv.at[1, face])
        await_bytes(local.at[face], SLOTS, face_send.at[1, face])

    def add_faces(s, carry):
        local[s // 4, lax.rem(s, 4)] = local[s // 4, lax.rem(s, 4)] + used(s) * got_local[s // 4, lax.rem(s, 4)]
        return carry

    lax.fori_loop(0, BLOCKS, add_faces, 0)
    loads[9].wait()

    await_bytes(e_got, ROWS - 1, recv_sem.at[7])
    loads[11].wait()
    coarse[...] = jnp.sum(e_got[...], axis=0)
    precond_dot = coarse[40:41]
    mix = precond_dot / prev_dot[...]

    for face in range(4):
        stack = jnp.concatenate([coarse[0:8], coarse[8 + 8 * face : 16 + 8 * face]], axis=0)
        high, low = split(stack)
        high = high.astype(F32)
        right = jnp.concatenate([high, low.astype(F32), high, jnp.zeros((80, CASES), F32)], axis=0).astype(BF16)
        for k in range(SLOTS):
            s = face * 4 + k
            value = local[face, k] + mm(lifted[s], right) + mix * previous[sigma[s]]
            direct[s] = value
            tiles_hl[s] = tile(value)

    total = jnp.zeros((8, CASES), F32)
    for face in (2, 3, 0, 1):
        def image_row(k, total):
            s = face * 4 + k
            both = mm(stiff[s, :, 0:256], tiles_hl[slot_pat[s, 0]])
            both = both + mm(stiff[s, :, 256:512], tiles_hl[slot_pat[s, 1]])
            both = both + mm(stiff[s, :, 512:768], tiles_hl[slot_pat[s, 2]])
            row = both[:, 0:CASES] + both[:, CASES:]
            image[face, k] = row
            return total + jnp.sum((direct[s] * row).reshape(16, 8, CASES), axis=0)

        total = lax.fori_loop(0, SLOTS, image_row, total, unroll=True)

    v_buf[j] = jnp.sum(total, axis=0, keepdims=True)
    push(v_buf.at[j], v_buf.at[j], col_ids, 8)
    for face in (2, 3):
        send_part(face, 0, 3)
    for face in (0, 1):
        send_part(face, 0, 4)

    def order_direction(b, carry):
        out_dir[b] = direct[place[b]]
        return carry

    lax.fori_loop(0, BLOCKS, order_direction, 0)
    loads[10].wait()

    await_bytes(v_buf, COLS - 1, recv_sem.at[8])
    w_own[...] = jnp.sum(v_buf[...], axis=0)
    w_got[i] = w_own[...]
    push(w_own, w_got.at[i], row_ids, 9)
    for face in (2, 3):
        send_part(face, 3, 1)

    for face in range(4):
        await_bytes(got_image.at[face], SLOTS, face_recv.at[2, face])

    def order_image(b, carry):
        s = place[b]
        out_image[b] = image[s // 4, lax.rem(s, 4)] + used(s) * got_image[s // 4, lax.rem(s, 4)]
        return carry

    lax.fori_loop(0, BLOCKS, order_image, 0)

    for buffer, count, stage in (
        (map_got, 7, 0), (a_buf, 7, 1), (map_got, 24, 2), (a_buf, 24, 3), (near_got, 7, 4), (b_got, 7, 5),
        (c_buf, 31, 6), (e_got, 7, 7), (v_buf, 31, 8),
    ):
        await_bytes(buffer, count, send_sem.at[stage])
    for face in range(4):
        await_bytes(face_basis.at[face], SLOTS, face_send.at[0, face])
        await_bytes(image.at[face], SLOTS, face_send.at[2, face])

    await_bytes(w_got, ROWS - 1, recv_sem.at[9])
    step[...] = precond_dot / jnp.sum(w_got[...], axis=0)

    await_bytes(w_got, ROWS - 1, send_sem.at[9])


def deliver(
    solution, residual, image, direction, step, new_solution, new_residual, new_direction,
    moved, left, sem,
):
    copies = [pltpu.make_async_copy(direction, new_direction, sem.at[0, 0])]
    copies[0].start()
    step_rows = jnp.broadcast_to(step[...], (DOFS, CASES))
    for part in range(CHUNKS):
        blocks = pl.ds(part * (BLOCKS // CHUNKS), BLOCKS // CHUNKS)
        for b in range(part * (BLOCKS // CHUNKS), (part + 1) * (BLOCKS // CHUNKS)):
            moved[b] = solution[b] + step_rows * direction[b]
            left[b] = residual[b] - step_rows * image[b]
        for n, (source, target) in enumerate(((moved, new_solution), (left, new_residual))):
            copies.append(pltpu.make_async_copy(source.at[blocks], target.at[blocks], sem.at[n + 1, part]))
            copies[-1].start()
    for copy in copies:
        copy.wait()


def per_device(
    solution, residual, prev_direction, prev_dot, face_lists, multiplicity, block_pattern,
    schur, neumann_inverse, coarse_basis, primal_map, coarse_inverse,
):
    field = jax.ShapeDtypeStruct((BLOCKS, DOFS, CASES), F32)
    hbm = pl.BlockSpec(memory_space=pltpu.HBM)
    vmem = pl.BlockSpec(memory_space=pltpu.VMEM)
    V = pltpu.VMEM
    tall = (4, SLOTS, DOFS, CASES)
    outs = pl.pallas_call(
        iteration,
        out_shape=(pltpu.VMEM((BLOCKS, DOFS, CASES), F32),) * 4 + (pltpu.VMEM((1, CASES), F32),),
        in_specs=[hbm] * 12,
        out_specs=(vmem,) * 5,
        scratch_shapes=[
            pltpu.SMEM((4, 4), jnp.int32), pltpu.SMEM((3, 1, 16), jnp.int32), pltpu.SMEM((1, 16), jnp.int32),
            pltpu.SMEM((1, 8), jnp.int32), V((1, 128), F32),
            pltpu.SMEM((16,), jnp.int32), pltpu.SMEM((16,), jnp.int32), pltpu.SMEM((16,), jnp.int32),
            pltpu.SMEM((16, 3), jnp.int32),
            V((16, 128, 128), F32),
            V((16, 3, 128, 128), F32), V((16, 3, 128, 128), F32), V((8, 2048), F32), V((16, 8, 128), F32), V((32, 1024), F32),
            V((16, 128, 256), BF16), V(tall, F32), V((16, 128, 768), BF16),
            V((16, 128, 128), BF16), V((128, 256), BF16), V((256, 256), BF16),
            V((16, 128, 128), F32), V((16, 256, 256), BF16), V(tall, F32),
            V((32, 1, 128), F32), V((1, 128), F32), V((8, 1, 128), F32),
            V((4, 4, 8, 128), F32), V((4, 4, 8, 128), F32), V(tall, F32), V(tall, F32),
            V((32, 8, 128), F32), V((8, 8, 128), F32), V((8, 8, 128), F32), V((32, 1, 640), F32),
            V((8, 48, 128), F32), V((8, 48, 128), F32), V((48, 128), F32), V((32, 1, 128), F32),
            V((1, 128), F32), V((8, 1, 128), F32),
            pltpu.SemaphoreType.DMA((12,)), pltpu.SemaphoreType.DMA((4,)), pltpu.SemaphoreType.DMA((10,)),
            pltpu.SemaphoreType.DMA((10,)), pltpu.SemaphoreType.DMA((3, 4)), pltpu.SemaphoreType.DMA((3, 4)),
        ],
        compiler_params=pltpu.CompilerParams(
            collective_id=0, has_side_effects=True, vmem_limit_bytes=48 * 1024 * 1024
        ),
        name="iteration",
    )(*(pltpu.with_memory_space_constraint(value, pltpu.HBM) for value in (
        face_lists[0, 0], jnp.transpose(block_pattern, (0, 3, 1, 2))[0], multiplicity[0], primal_map[0],
        prev_dot.reshape(1, CASES), residual[0, 0], prev_direction[0, 0], solution[0, 0],
        schur[0, 0], neumann_inverse[0, 0], coarse_basis[0, 0], coarse_inverse,
    )))
    outs = pl.pallas_call(
        deliver,
        out_shape=(field, field, field),
        in_specs=[vmem] * 5,
        out_specs=(hbm, hbm, hbm),
        scratch_shapes=[
            pltpu.VMEM((BLOCKS, DOFS, CASES), F32), pltpu.VMEM((BLOCKS, DOFS, CASES), F32),
            pltpu.SemaphoreType.DMA((3, CHUNKS)),
        ],
        compiler_params=pltpu.CompilerParams(vmem_limit_bytes=4 * 1024 * 1024),
        name="deliver",
    )(*outs)
    return tuple(out[None, None] for out in outs)


def solution(mesh):
    field = P("row", "col", None, None, None)
    return jax.shard_map(
        per_device,
        mesh=mesh,
        in_specs=(
            field, field, field, P(), P("row", "col", None, None), P("row", "col", None), P("row", "col", None, None),
            P("row", "col", None, None, None, None), P("row", "col", None, None, None, None),
            P("row", "col", None, None), P("row", "col", None), P("col", None),
        ),
        out_specs=(field, field, field),
        check_vma=False,
    )
```

```python
import jax
import jax.numpy as jnp
from jax import lax
from jax.experimental import pallas as pl
from jax.experimental.pallas import tpu as pltpu
from jax.sharding import PartitionSpec as P

MESH = pl.DeviceIdType.MESH
F32 = jnp.float32
BF16 = jnp.bfloat16
ROWS, COLS = 8, 32
BLOCKS, DOFS, CASES, SLOTS, PRIMALS = 16, 128, 128, 4, 8
CHUNKS = 4
OWNED = 32
COARSE = OWNED * COLS
OPPOSITE = (1, 0, 3, 2)


def split(values):
    high = values.astype(BF16)
    return high, (values - high.astype(F32)).astype(BF16)


def mm(left, right):
    return jnp.dot(left, right, preferred_element_type=F32)


def wide(values):
    return jnp.concatenate(split(values), axis=1)


def tile(values):
    high, low = split(values)
    top = jnp.concatenate([high, low], axis=1)
    return jnp.concatenate([top, jnp.concatenate([high, jnp.zeros_like(low)], axis=1)], axis=0)


def iteration(
    faces_h, pattern_h, mult_h, pmap_h, prev_dot_h,
    residual_h, previous_h, solution_h, schur_h, neumann_h, basis_h, inverse_h,
    solution, residual, out_image, out_dir, step,
    faces, pattern, mult, pmap, prev_dot,
    nonface, sigma, place, slot_pat,
    previous, schur, neumann, basis, tiles, inverse,
    scaled, local, stiff, lifted, chosen, picker,
    direct, tiles_hl, image,
    map_got, near_own, near_got,
    face_basis, got_basis, got_local, got_image,
    a_buf, b_own, b_got, c_buf, e_own, e_got, coarse, v_buf, w_own, w_got,
    load_sem, part_sem, send_sem, recv_sem, face_send, face_recv,
):
    i = lax.axis_index("row")
    j = lax.axis_index("col")
    z, x = j // 4, lax.rem(j, 4)
    row_id = lambda t: (lax.rem(i + t, ROWS), j)
    col_id = lambda t: (i, lax.rem(j + t, COLS))
    face_id = (row_id(ROWS - 1), row_id(1), col_id(COLS - 1), col_id(1))
    z_at = [lax.rem(z + t, 8) * 4 for t in range(8)]
    x_at = [lax.rem(x + t, 4) for t in range(4)]
    z_far, x_far = (4, 3, 5, 2, 6, 1, 7), (2, 1, 3)
    z_ids = [(i, z_at[t] + x) for t in z_far]
    x_ids = [(i, z * 4 + x_at[t]) for t in x_far]
    hops = lambda t: min(t[0], 8 - t[0]) + min(t[1], 4 - t[1])
    offsets = sorted(((dz, dx) for dz in range(8) for dx in range(4) if dz or dx), key=lambda t: (-min(t[0], 8 - t[0]), -min(t[1], 4 - t[1])))
    col_ids = [(i, z_at[dz] + x_at[dx]) for dz, dx in offsets]
    row_ids = [row_id(t) for t in (4, 5, 3, 6, 2, 7, 1)]

    pairs = (
        (faces_h, faces), (pattern_h, pattern), (mult_h, mult), (pmap_h, pmap),
        (residual_h, residual), (basis_h, basis), (inverse_h, inverse), (neumann_h, neumann),
        (schur_h, schur), (previous_h, previous), (solution_h, solution), (prev_dot_h, prev_dot),
    )
    loads = [pltpu.make_async_copy(source, target, load_sem.at[n]) for n, (source, target) in enumerate(pairs)]
    parts = [
        pltpu.make_async_copy(residual_h.at[pl.ds(4 * n, 4)], residual.at[pl.ds(4 * n, 4)], part_sem.at[n]) for n in range(4)
    ]
    loads[5].start()
    parts[0].start()
    loads[2].start()
    for n in range(1, 4):
        parts[n].start()
    for n in (3, 0, 1):
        loads[n].start()

    barrier = pltpu.get_barrier_semaphore()
    for peer in z_ids + x_ids + row_ids:
        pl.semaphore_signal(barrier, inc=1, device_id=peer, device_id_type=MESH)
    loads[7].start()
    loads[6].start()

    def push(source, target, peers, stage):
        for peer in peers:
            pltpu.make_async_remote_copy(
                src_ref=source, dst_ref=target, send_sem=send_sem.at[stage], recv_sem=recv_sem.at[stage],
                device_id=peer, device_id_type=MESH,
            ).start()

    def scatter_row(own, got, stage):
        for t in (4, 5, 3, 6, 2, 7, 1):
            pltpu.make_async_remote_copy(
                src_ref=own.at[lax.rem(i + t, ROWS)], dst_ref=got.at[i],
                send_sem=send_sem.at[stage], recv_sem=recv_sem.at[stage],
                device_id=row_id(t), device_id_type=MESH,
            ).start()

    def await_bytes(buffer, count, sem):
        view = buffer.at[pl.ds(0, count)]
        pltpu.make_async_copy(view, view, sem).wait()

    def send_face(own, got, face, group):
        pltpu.make_async_remote_copy(
            src_ref=own, dst_ref=got.at[OPPOSITE[face]],
            send_sem=face_send.at[group, face], recv_sem=face_recv.at[group, OPPOSITE[face]],
            device_id=face_id[face], device_id_type=MESH,
        ).start()

    loads[2].wait()
    weight = lambda b: jnp.where(mult[0, b] == 2, F32(0.5), F32(1.0))
    used = lambda s: jnp.where(faces[s // 4, s % 4] < BLOCKS, F32(1.0), F32(0.0))

    lanes = lax.broadcasted_iota(jnp.int32, (1, 128), 1)
    home = x * 8 + z

    loads[5].wait()

    both = jnp.zeros((16, 2 * CASES), F32)
    for b in range(0, BLOCKS, 2):
        if b % 4 == 0:
            parts[b // 4].wait()
        for n in (b, b + 1):
            scaled[n] = wide(residual[n] * weight(n))
        left = jnp.concatenate(split(basis[:, b * DOFS : (b + 2) * DOFS]), axis=0)
        both = both + mm(left, scaled[pl.ds(b, 2)].reshape(2 * DOFS, 2 * CASES))
    a_buf[home] = both[0:8, 0:CASES] + both[0:8, CASES:] + both[8:16, 0:CASES]

    loads[3].wait()
    own_map = jnp.zeros((1, 128), jnp.int32)
    for p in range(PRIMALS):
        own_map = jnp.where(lax.rem(lanes, 8) == p, pmap[0, p], own_map)
    map_got[home] = own_map.astype(F32)
    pl.semaphore_wait(barrier, 17)
    push(map_got.at[home], map_got.at[home], z_ids, 0)
    push(a_buf.at[home], a_buf.at[home], z_ids, 1)
    for n in (8, 9, 10, 11):
        loads[n].start()

    for n in (0, 1):
        loads[n].wait()

    def send_part(face, first, count):
        part = pl.ds(first, count)
        pltpu.make_async_remote_copy(
            src_ref=image.at[face, part], dst_ref=got_image.at[OPPOSITE[face], part],
            send_sem=face_send.at[2, face], recv_sem=face_recv.at[2, OPPOSITE[face]],
            device_id=face_id[face], device_id_type=MESH,
        ).start()

    def find_nonface(b, count):
        on_face = faces[0, 0] == b
        for s in range(1, 16):
            on_face = jnp.logical_or(on_face, faces[s // 4, s % 4] == b)
        nonface[b] = jnp.where(on_face, -1, count)
        return count + jnp.where(on_face, 0, 1)

    lax.fori_loop(0, BLOCKS, find_nonface, jnp.int32(0))

    def find_sigma(s, count):
        named = faces[s // 4, s % 4]
        free = named >= BLOCKS
        block = jnp.int32(0)
        for b in range(BLOCKS):
            block = jnp.where(nonface[b] == count, b, block)
        sigma[s] = jnp.where(free, block, named)
        return count + jnp.where(free, 1, 0)

    lax.fori_loop(0, BLOCKS, find_sigma, jnp.int32(0))

    def find_place(b, carry):
        slot = jnp.int32(0)
        for s in range(BLOCKS):
            slot = jnp.where(sigma[s] == b, s, slot)
        place[b] = slot
        return carry

    lax.fori_loop(0, BLOCKS, find_place, 0)

    def find_slot_pat(s, carry):
        for k in range(3):
            slot_pat[s, k] = place[pattern[k, 0, sigma[s]]]
        return carry

    lax.fori_loop(0, BLOCKS, find_slot_pat, 0)

    for b in range(BLOCKS):
        tiles[b] = basis[:, b * DOFS : (b + 1) * DOFS]
    for face in (2, 3, 0, 1):
        for k in range(SLOTS):
            b = sigma[face * 4 + k]
            face_basis[face, k] = tiles[b]

    loads[7].wait()

    def local_row(s, dot):
        b = sigma[s]
        blocks = jnp.concatenate([neumann[b, k] for k in range(3)], axis=1)
        high, low = split(blocks)
        values = jnp.concatenate([scaled[pattern[k, 0, b]] for k in range(3)], axis=0)
        both = mm(high, values)
        row = both[:, 0:CASES] + both[:, CASES:] + mm(low, values[:, 0:CASES])
        row = row * weight(b)
        local[s // 4, lax.rem(s, 4)] = row
        return dot + jnp.sum((residual[b] * row).reshape(16, 8, CASES), axis=0)

    local_dot = lax.fori_loop(0, BLOCKS, local_row, jnp.zeros((8, CASES), F32), unroll=2)
    local_dot = jnp.sum(local_dot, axis=0, keepdims=True)
    line_of = lambda buffer: buffer.at[pl.ds(x * 8, 8)]
    await_bytes(map_got, 7, recv_sem.at[0])
    push(line_of(map_got), line_of(map_got), x_ids, 2)
    await_bytes(a_buf, 7, recv_sem.at[1])
    push(line_of(a_buf), line_of(a_buf), x_ids, 3)
    for face in (2, 3, 0, 1):
        send_face(face_basis.at[face], got_basis, face, 0)

    await_bytes(map_got, 24, recv_sem.at[2])
    group = lanes // 8
    code = jnp.where(lax.rem(lanes, 8) == 0, F32(-1.0), F32(-2.0))
    before, after = lax.rem(j + COLS - 1, COLS), lax.rem(j + 1, COLS)
    west = map_got[lax.rem(before, 4) * 8 + before // 4]
    east = map_got[lax.rem(after, 4) * 8 + after // 4]
    quarter = lax.rem(group, 4)
    near_own[...] = jnp.where(quarter == 0, map_got[home], jnp.where(quarter == 1, west, jnp.where(quarter == 2, east, code)))
    near_got[i] = near_own[...]
    push(near_own, near_got.at[i], row_ids, 4)
    halves = []
    for half in range(2):
        line = jnp.zeros((1, 128), F32)
        for t in range(16):
            line = jnp.where(group == t, map_got[half * 16 + t], line)
        halves.append(line.astype(jnp.int32))
    entries = jnp.concatenate(halves, axis=1)
    loads[6].wait()

    def pick(c, total):
        rows = lax.broadcasted_iota(jnp.int32, (256, 256), 0) + c * 256
        hot = jnp.where(rows == entries, F32(1.0), F32(0.0)).astype(BF16)
        return total + mm(wide_rows(inverse[:, pl.ds(pl.multiple_of(c * 256, 256), 256)]), hot)

    wide_rows = lambda values: jnp.concatenate(split(values), axis=0)
    total = lax.fori_loop(0, COARSE // 256, pick, jnp.zeros((2 * OWNED, 256), F32))
    columns_hi, columns_lo = split(total[0:OWNED] + total[OWNED:])
    rows = lax.broadcasted_iota(jnp.int32, (64, OWNED), 0)
    cols = lax.broadcasted_iota(jnp.int32, (64, OWNED), 1)
    spot = (rows // 8) * 4 + lax.rem(rows, 4)
    first = lax.rem(rows, 8) < 4
    order = jnp.where(jnp.logical_and(first, spot == cols), F32(1.0), F32(0.0)).astype(BF16)
    rows = lax.broadcasted_iota(jnp.int32, (64, 256), 0)
    spot = (rows // 8) * 4 + lax.rem(rows, 4) + j * OWNED
    first = lax.rem(rows, 8) < 4
    own_hot = jnp.where(jnp.logical_and(jnp.logical_not(first), spot == entries), F32(1.0), F32(0.0))
    chosen[0:64] = (mm(order, columns_hi) + own_hot).astype(BF16)
    chosen[64:128] = mm(order, columns_lo).astype(BF16)

    await_bytes(a_buf, 24, recv_sem.at[3])
    both = mm(chosen[...], wide(a_buf[...].reshape(COLS * PRIMALS, CASES)))
    parts = both[0:64, 0:CASES] + both[0:64, CASES:] + both[64:128, 0:CASES]
    b_own[...] = parts.reshape(ROWS, 8, CASES)
    b_got[i] = b_own[i]
    scatter_row(b_own, b_got, 5)

    await_bytes(near_got, ROWS - 1, recv_sem.at[4])
    for half in range(2):
        line = jnp.zeros((1, 128), F32)
        for t in range(4):
            line = jnp.where(lanes // 32 == t, near_got[half * 4 + t], line)
        line = line.astype(jnp.int32)
        here = jnp.logical_and(line >= 0, lax.rem(line // 4, 8) == i)
        where_at = jnp.where(here, lax.rem(line, 4) * COLS + line // OWNED, -1)
        for quarter_rows in range(2):
            rows = lax.broadcasted_iota(jnp.int32, (128, 128), 0) + quarter_rows * 128
            hit = jnp.logical_or(rows == where_at, jnp.logical_and(line == -1, rows // COLS == 4))
            hot = jnp.where(hit, F32(1.0), F32(0.0))
            picker[pl.ds(half * 128, 128), pl.ds(quarter_rows * 128, 128)] = jnp.transpose(hot).astype(BF16)

    await_bytes(b_got, ROWS - 1, recv_sem.at[5])
    held = jnp.sum(b_got[...], axis=0)
    dot = 0.5 * jnp.sum(held * pltpu.roll(held, 4, 0), axis=0, keepdims=True) + local_dot
    for q in range(4):
        c_buf[j, :, q * CASES : (q + 1) * CASES] = held[q : q + 1]
    c_buf[j, :, 4 * CASES :] = dot
    push(c_buf.at[j], c_buf.at[j], col_ids, 6)
    for face in (2, 3, 0, 1):
        send_face(local.at[face], got_local, face, 1)

    loads[8].wait()

    def order_schur(s, carry):
        b = sigma[s]
        for k in range(3):
            stiff[s, :, 2 * k * DOFS : 2 * (k + 1) * DOFS] = wide(schur[b, k])
        return carry

    lax.fori_loop(0, BLOCKS, order_schur, 0)

    for face in range(4):
        await_bytes(got_basis.at[face], SLOTS, face_recv.at[0, face])

    def lift(s, carry):
        b = sigma[s]
        own = tiles[b]
        other = got_basis[s // 4, lax.rem(s, 4)] * used(s)
        stack = jnp.concatenate([own, other], axis=0) * weight(b)
        high, low = split(stack)
        high = high.astype(F32)
        full = jnp.concatenate([high, high, low.astype(F32), jnp.zeros((80, DOFS), F32)], axis=0)
        lifted[s] = jnp.transpose(full).astype(BF16)
        return carry

    lax.fori_loop(0, BLOCKS, lift, 0)

    await_bytes(c_buf, COLS - 1, recv_sem.at[6])
    rows_held = [c_buf[:, :, q * CASES : (q + 1) * CASES].reshape(COLS, CASES) for q in range(5)]
    both = mm(picker[...], wide(jnp.concatenate(rows_held + [jnp.zeros((96, CASES), F32)], axis=0)))
    rows_for = both[:, 0:CASES] + both[:, CASES:]
    for t in range(ROWS):
        north, south = (t + 7) % ROWS * 32, (t + 1) % ROWS * 32
        e_own[t, 0:8] = rows_for[t * 32 : t * 32 + 8]
        e_own[t, 8:16] = rows_for[north : north + 8]
        e_own[t, 16:24] = rows_for[south : south + 8]
        e_own[t, 24:48] = rows_for[t * 32 + 8 : t * 32 + 32]
    e_got[i] = e_own[i]
    scatter_row(e_own, e_got, 7)
    for face in range(4):
        await_bytes(got_local.at[face], SLOTS, face_recv.at[1, face])
        await_bytes(local.at[face], SLOTS, face_send.at[1, face])

    def add_faces(s, carry):
        local[s // 4, lax.rem(s, 4)] = local[s // 4, lax.rem(s, 4)] + used(s) * got_local[s // 4, lax.rem(s, 4)]
        return carry

    lax.fori_loop(0, BLOCKS, add_faces, 0)
    loads[9].wait()

    await_bytes(e_got, ROWS - 1, recv_sem.at[7])
    loads[11].wait()
    coarse[...] = jnp.sum(e_got[...], axis=0)
    precond_dot = coarse[40:41]
    mix = precond_dot / prev_dot[...]

    for face in range(4):
        stack = jnp.concatenate([coarse[0:8], coarse[8 + 8 * face : 16 + 8 * face]], axis=0)
        high, low = split(stack)
        high = high.astype(F32)
        right = jnp.concatenate([high, low.astype(F32), high, jnp.zeros((80, CASES), F32)], axis=0).astype(BF16)
        for k in range(SLOTS):
            s = face * 4 + k
            value = local[face, k] + mm(lifted[s], right) + mix * previous[sigma[s]]
            direct[s] = value
            tiles_hl[s] = tile(value)

    total = jnp.zeros((8, CASES), F32)
    for face in (2, 3, 0, 1):
        def image_row(k, total):
            s = face * 4 + k
            both = mm(stiff[s, :, 0:256], tiles_hl[slot_pat[s, 0]])
            both = both + mm(stiff[s, :, 256:512], tiles_hl[slot_pat[s, 1]])
            both = both + mm(stiff[s, :, 512:768], tiles_hl[slot_pat[s, 2]])
            row = both[:, 0:CASES] + both[:, CASES:]
            image[face, k] = row
            return total + jnp.sum((direct[s] * row).reshape(16, 8, CASES), axis=0)

        total = lax.fori_loop(0, SLOTS, image_row, total, unroll=True)

    v_buf[j] = jnp.sum(total, axis=0, keepdims=True)
    push(v_buf.at[j], v_buf.at[j], col_ids, 8)
    for face in (2, 3):
        send_part(face, 0, 3)
    for face in (0, 1):
        send_part(face, 0, 4)

    def order_direction(b, carry):
        out_dir[b] = direct[place[b]]
        return carry

    lax.fori_loop(0, BLOCKS, order_direction, 0)
    loads[10].wait()

    await_bytes(v_buf, COLS - 1, recv_sem.at[8])
    w_own[...] = jnp.sum(v_buf[...], axis=0)
    w_got[i] = w_own[...]
    push(w_own, w_got.at[i], row_ids, 9)
    for face in (2, 3):
        send_part(face, 3, 1)

    for face in range(4):
        await_bytes(got_image.at[face], SLOTS, face_recv.at[2, face])

    def order_image(b, carry):
        s = place[b]
        out_image[b] = image[s // 4, lax.rem(s, 4)] + used(s) * got_image[s // 4, lax.rem(s, 4)]
        return carry

    lax.fori_loop(0, BLOCKS, order_image, 0)

    for buffer, count, stage in (
        (map_got, 7, 0), (a_buf, 7, 1), (map_got, 24, 2), (a_buf, 24, 3), (near_got, 7, 4), (b_got, 7, 5),
        (c_buf, 31, 6), (e_got, 7, 7), (v_buf, 31, 8),
    ):
        await_bytes(buffer, count, send_sem.at[stage])
    for face in range(4):
        await_bytes(face_basis.at[face], SLOTS, face_send.at[0, face])
        await_bytes(image.at[face], SLOTS, face_send.at[2, face])

    await_bytes(w_got, ROWS - 1, recv_sem.at[9])
    step[...] = precond_dot / jnp.sum(w_got[...], axis=0)

    await_bytes(w_got, ROWS - 1, send_sem.at[9])


def deliver(
    solution, residual, image, direction, step, new_solution, new_residual, new_direction,
    moved, left, sem,
):
    copies = [pltpu.make_async_copy(direction, new_direction, sem.at[0, 0])]
    copies[0].start()
    step_rows = jnp.broadcast_to(step[...], (DOFS, CASES))
    for part in range(CHUNKS):
        blocks = pl.ds(part * (BLOCKS // CHUNKS), BLOCKS // CHUNKS)
        for b in range(part * (BLOCKS // CHUNKS), (part + 1) * (BLOCKS // CHUNKS)):
            moved[b] = solution[b] + step_rows * direction[b]
            left[b] = residual[b] - step_rows * image[b]
        for n, (source, target) in enumerate(((moved, new_solution), (left, new_residual))):
            copies.append(pltpu.make_async_copy(source.at[blocks], target.at[blocks], sem.at[n + 1, part]))
            copies[-1].start()
    for copy in copies:
        copy.wait()


def per_device(
    solution, residual, prev_direction, prev_dot, face_lists, multiplicity, block_pattern,
    schur, neumann_inverse, coarse_basis, primal_map, coarse_inverse,
):
    field = jax.ShapeDtypeStruct((BLOCKS, DOFS, CASES), F32)
    hbm = pl.BlockSpec(memory_space=pltpu.HBM)
    vmem = pl.BlockSpec(memory_space=pltpu.VMEM)
    V = pltpu.VMEM
    tall = (4, SLOTS, DOFS, CASES)
    outs = pl.pallas_call(
        iteration,
        out_shape=(pltpu.VMEM((BLOCKS, DOFS, CASES), F32),) * 4 + (pltpu.VMEM((1, CASES), F32),),
        in_specs=[hbm] * 12,
        out_specs=(vmem,) * 5,
        scratch_shapes=[
            pltpu.SMEM((4, 4), jnp.int32), pltpu.SMEM((3, 1, 16), jnp.int32), pltpu.SMEM((1, 16), jnp.int32),
            pltpu.SMEM((1, 8), jnp.int32), V((1, 128), F32),
            pltpu.SMEM((16,), jnp.int32), pltpu.SMEM((16,), jnp.int32), pltpu.SMEM((16,), jnp.int32),
            pltpu.SMEM((16, 3), jnp.int32),
            V((16, 128, 128), F32),
            V((16, 3, 128, 128), F32), V((16, 3, 128, 128), F32), V((8, 2048), F32), V((16, 8, 128), F32), V((32, 1024), F32),
            V((16, 128, 256), BF16), V(tall, F32), V((16, 128, 768), BF16),
            V((16, 128, 128), BF16), V((128, 256), BF16), V((256, 256), BF16),
            V((16, 128, 128), F32), V((16, 256, 256), BF16), V(tall, F32),
            V((32, 1, 128), F32), V((1, 128), F32), V((8, 1, 128), F32),
            V((4, 4, 8, 128), F32), V((4, 4, 8, 128), F32), V(tall, F32), V(tall, F32),
            V((32, 8, 128), F32), V((8, 8, 128), F32), V((8, 8, 128), F32), V((32, 1, 640), F32),
            V((8, 48, 128), F32), V((8, 48, 128), F32), V((48, 128), F32), V((32, 1, 128), F32),
            V((1, 128), F32), V((8, 1, 128), F32),
            pltpu.SemaphoreType.DMA((12,)), pltpu.SemaphoreType.DMA((4,)), pltpu.SemaphoreType.DMA((10,)),
            pltpu.SemaphoreType.DMA((10,)), pltpu.SemaphoreType.DMA((3, 4)), pltpu.SemaphoreType.DMA((3, 4)),
        ],
        compiler_params=pltpu.CompilerParams(
            collective_id=0, has_side_effects=True, vmem_limit_bytes=48 * 1024 * 1024
        ),
        name="iteration",
    )(*(pltpu.with_memory_space_constraint(value, pltpu.HBM) for value in (
        face_lists[0, 0], jnp.transpose(block_pattern, (0, 3, 1, 2))[0], multiplicity[0], primal_map[0],
        prev_dot.reshape(1, CASES), residual[0, 0], prev_direction[0, 0], solution[0, 0],
        schur[0, 0], neumann_inverse[0, 0], coarse_basis[0, 0], coarse_inverse,
    )))
    outs = pl.pallas_call(
        deliver,
        out_shape=(field, field, field),
        in_specs=[vmem] * 5,
        out_specs=(hbm, hbm, hbm),
        scratch_shapes=[
            pltpu.VMEM((BLOCKS, DOFS, CASES), F32), pltpu.VMEM((BLOCKS, DOFS, CASES), F32),
            pltpu.SemaphoreType.DMA((3, CHUNKS)),
        ],
        compiler_params=pltpu.CompilerParams(vmem_limit_bytes=4 * 1024 * 1024),
        name="deliver",
    )(*outs)
    return tuple(out[None, None] for out in outs)


def solution(mesh):
    field = P("row", "col", None, None, None)
    return jax.shard_map(
        per_device,
        mesh=mesh,
        in_specs=(
            field, field, field, P(), P("row", "col", None, None), P("row", "col", None), P("row", "col", None, None),
            P("row", "col", None, None, None, None), P("row", "col", None, None, None, None),
            P("row", "col", None, None), P("row", "col", None), P("col", None),
        ),
        out_specs=(field, field, field),
        check_vma=False,
    )
```
